128 devices in a mesh: rows: 16 (over z, y_hi, core), grp: 8 (over y_lo, x).
Axes of the slice: x: 4, y: 4 (y_hi: 2, y_lo: 2; y = y_hi * 2 + y_lo), z: 4, core: 2. Of those that a mesh axis runs over, the one named last changes fastest.
Arguments:
- sorted_rows: bfloat16 [32768, 2048], P(('rows', 'grp')), may hold values from -6 to 6
- combine: bfloat16 [32768], P(('rows', 'grp')), may hold values from 0.099609375 to 1
- cotangent: bfloat16 [32768, 2048], P(('rows', 'grp')), may hold values from -6 to 6
- starts: int32 [128], P(('rows', 'grp')), may hold values from 0 to 32767, as said below
- w_gate: bfloat16 [128, 2048, 768], P(('rows', 'grp')), may hold values from -0.125 to 0.125
- w_up: bfloat16 [128, 2048, 768], P(('rows', 'grp')), may hold values from -0.125 to 0.125
- w_down: bfloat16 [128, 768, 2048], P(('rows', 'grp')), may hold values from -0.21875 to 0.21875
Outputs:
- mixed: bfloat16 [32768, 2048], P(('rows', 'grp'))
- combine_grad: bfloat16 [32768], P(('rows', 'grp'))
- input_grad: bfloat16 [32768, 2048], P(('rows', 'grp'))
- grad_gate: bfloat16 [128, 2048, 768], P(('rows', 'grp'))
- grad_up: bfloat16 [128, 2048, 768], P(('rows', 'grp'))
- grad_down: bfloat16 [128, 768, 2048], P(('rows', 'grp'))
The draws below stay inside these ranges and needn't reach their ends.
Inputs may be any that keep to these rules, and one draw needn't show every extreme that they name: starts[e] is the first sorted row of expert e; starts[0] = 0, starts[127] = 32767, and 256 * e < starts[e] < 256 * (e + 1) for e >= 1, so the rows of expert e lie in shards e and e + 1 of 256 rows, and every shard after the first begins with rows of the previous expert.
All inputs are finite; a program needn't handle non-finite values.
Results may differ from the reference program's by a relative error of at most 0.0058.
Values may be sent and summed in bfloat16 or wider, within the bound.
A program may use at most 128 MiB of HBM per device.

```python
import math
import jax
import jax.numpy as jnp
from jax import lax

D = 2048
H = 768
ROW_DEV = 256
EXPERTS = 128
ROWS = 32768


def draw_starts(key, part):
    expert_pos = jnp.arange(EXPERTS, dtype=jnp.int32)
    offsets = jax.random.randint(key, (EXPERTS,), 1, ROW_DEV, dtype=jnp.int32)
    offsets = jnp.where(expert_pos == 0, jnp.zeros_like(offsets), offsets)
    offsets = jnp.where(expert_pos == EXPERTS - 1, jnp.full_like(offsets, ROW_DEV - 1), offsets)
    return (expert_pos * ROW_DEV + offsets).astype(jnp.int32)


def shard_levels(own_key, dims, shards, smallest, top_value):
    factor_of, own = 1.0, jax.random.fold_in(own_key, 6)
    for position, blocks in shards:
        heights = jnp.exp(jax.random.uniform(jax.random.fold_in(own, position), (blocks,), jnp.float32, smallest / len(shards), top_value / len(shards)))
        factor_of = factor_of * jnp.repeat(heights, dims[position] // blocks).reshape([-1 if axis == position else 1 for axis in range(len(dims))])
    return factor_of


def normal_values(key, extent, width, bound, shards=(), held_as=jnp.bfloat16):
    level = shard_levels(key, extent, shards, -0.22, 0.18) if shards else 1.0
    array = jax.random.normal(key, extent, jnp.float32) * width * level
    return jnp.minimum(jnp.maximum(array, -bound), bound).astype(held_as)


def setup_inputs(seed: int = 0) -> dict:
    key_of = jax.random.split(jax.random.key(seed), 8)
    return {
        "sorted_rows": normal_values(key_of[0], (ROWS, D), 1.0, 6.0, ((0, 128),)),
        "combine": jnp.clip(jnp.exp(math.log(1.0) - 2.306499 * jax.random.uniform(key_of[1], (ROWS,), jnp.float32) ** shard_levels(key_of[1], (ROWS,), ((0, 128),), -0.2, 0.2)), 0.099609375, 1.0).astype(jnp.bfloat16),
        "cotangent": normal_values(key_of[2], (ROWS, D), 1.0, 6.0, ((0, 128),)),
        "starts": draw_starts(jax.random.fold_in(key_of[7], 71), 0),
        "w_gate": normal_values(key_of[4], (EXPERTS, D, H), D ** -0.5, 0.125, ((0, 128),)),
        "w_up": normal_values(key_of[5], (EXPERTS, D, H), D ** -0.5, 0.125, ((0, 128),)),
        "w_down": normal_values(key_of[6], (EXPERTS, H, D), H ** -0.5, 0.21875, ((0, 128),)),
    }


def expert_forward(rows_in, combine_rows, cotan_rows, gate_w, up_w, down_w):
    gate_pre = jnp.dot(rows_in, gate_w, preferred_element_type=jnp.float32)
    up_pre = jnp.dot(rows_in, up_w, preferred_element_type=jnp.float32)
    sig_gate = jax.nn.sigmoid(gate_pre)
    silu_gate = gate_pre * sig_gate
    hidden = (silu_gate * up_pre).astype(jnp.bfloat16)
    expert_out = jnp.dot(hidden, down_w, preferred_element_type=jnp.float32)
    scale_col = combine_rows.astype(jnp.float32)[:, None]
    mixed = (scale_col * expert_out).astype(jnp.bfloat16)
    comb_grad = jnp.sum(expert_out * cotan_rows.astype(jnp.float32), axis=1).astype(jnp.bfloat16)
    out_grad = (scale_col * cotan_rows.astype(jnp.float32)).astype(jnp.bfloat16)
    return gate_pre, up_pre, sig_gate, silu_gate, hidden, mixed, comb_grad, out_grad


def expert_backward(rows_in, out_grad, gate_pre, up_pre, sig_gate, silu_gate, hidden, gate_w, up_w, down_w):
    hidden_grad = jnp.dot(out_grad, down_w.T, preferred_element_type=jnp.float32)
    gate_grad = (hidden_grad * up_pre * sig_gate * (1.0 + gate_pre * (1.0 - sig_gate))).astype(jnp.bfloat16)
    up_grad = (hidden_grad * silu_gate).astype(jnp.bfloat16)
    in_grad = (jnp.dot(gate_grad, gate_w.T, preferred_element_type=jnp.float32)
               + jnp.dot(up_grad, up_w.T, preferred_element_type=jnp.float32)).astype(jnp.bfloat16)
    gate_wgrad = jnp.dot(rows_in.T, gate_grad, preferred_element_type=jnp.float32)
    up_wgrad = jnp.dot(rows_in.T, up_grad, preferred_element_type=jnp.float32)
    down_wgrad = jnp.dot(hidden.T, out_grad, preferred_element_type=jnp.float32)
    return in_grad, gate_wgrad, up_wgrad, down_wgrad


def join_halves(first, second):
    shifted = jnp.concatenate([jnp.zeros_like(second[:1]), second[:-1]], axis=0)
    total = first + shifted
    return total.reshape((ROWS,) + total.shape[2:])


def reference(sorted_rows, combine, cotangent, starts, w_gate, w_up, w_down):
    rows_ext = jnp.concatenate([sorted_rows, jnp.zeros((ROW_DEV, D), sorted_rows.dtype)], axis=0)
    cotan_ext = jnp.concatenate([cotangent, jnp.zeros((ROW_DEV, D), cotangent.dtype)], axis=0)
    comb_ext = jnp.concatenate([combine, jnp.zeros((ROW_DEV,), combine.dtype)], axis=0)
    bounds = jnp.concatenate([starts.astype(jnp.int32), jnp.full((1,), ROWS, jnp.int32)]).astype(jnp.int32)

    def one_expert(expert):
        base = (expert * ROW_DEV).astype(jnp.int32)
        rows_in = lax.dynamic_slice_in_dim(rows_ext, base, 2 * ROW_DEV, 0)
        cotan_rows = lax.dynamic_slice_in_dim(cotan_ext, base, 2 * ROW_DEV, 0)
        comb_rows = lax.dynamic_slice_in_dim(comb_ext, base, 2 * ROW_DEV, 0)
        index_rows = base + jnp.arange(2 * ROW_DEV, dtype=jnp.int32)
        member = (index_rows >= bounds[expert]) & (index_rows < bounds[expert + 1])
        gate_w = w_gate[expert]
        up_w = w_up[expert]
        down_w = w_down[expert]
        gate_pre, up_pre, sig_gate, silu_gate, hidden, mixed, comb_grad, out_grad = expert_forward(
            rows_in, comb_rows, cotan_rows, gate_w, up_w, down_w)
        out_grad = jnp.where(member[:, None], out_grad, jnp.zeros_like(out_grad))
        in_grad, gate_wgrad, up_wgrad, down_wgrad = expert_backward(
            rows_in, out_grad, gate_pre, up_pre, sig_gate, silu_gate, hidden, gate_w, up_w, down_w)
        mixed = jnp.where(member[:, None], mixed, jnp.zeros_like(mixed))
        comb_grad = jnp.where(member, comb_grad, jnp.zeros_like(comb_grad))
        in_grad = jnp.where(member[:, None], in_grad, jnp.zeros_like(in_grad))
        return (mixed[:ROW_DEV], mixed[ROW_DEV:], comb_grad[:ROW_DEV], comb_grad[ROW_DEV:],
                in_grad[:ROW_DEV], in_grad[ROW_DEV:], gate_wgrad.astype(jnp.bfloat16),
                up_wgrad.astype(jnp.bfloat16), down_wgrad.astype(jnp.bfloat16))

    results = lax.map(one_expert, jnp.arange(EXPERTS, dtype=jnp.int32))
    mixed = join_halves(results[0], results[1])
    comb_grad = join_halves(results[2], results[3])
    in_grad = join_halves(results[4], results[5])
    return mixed, comb_grad, in_grad, results[6], results[7], results[8]
```

```python
import jax
import jax.numpy as jnp
from jax import lax
from jax.sharding import PartitionSpec as P

AXES = ("rows", "grp")
X_CHUNKS = 2
C_CHUNKS = 4


def shift(block, distance):
    count = lax.axis_size(AXES)
    return lax.ppermute(block, AXES, [(i, (i + distance) % count) for i in range(count)])


def contract_rows(left, right):
    return lax.dot_general(
        left, right, (((0,), (0,)), ((), ())), preferred_element_type=jnp.float32
    )


def contract_cols(left, right):
    return lax.dot_general(
        left, right, (((1,), (1,)), ((), ())), preferred_element_type=jnp.float32
    )


def forward(rows_in, scale_col, gate_w, up_w, down_w):
    gate_pre = jnp.dot(rows_in, gate_w, preferred_element_type=jnp.float32)
    up_pre = jnp.dot(rows_in, up_w, preferred_element_type=jnp.float32)
    sig_gate = jax.nn.sigmoid(gate_pre)
    hidden = (gate_pre * sig_gate * up_pre).astype(jnp.bfloat16)
    expert_out = jnp.dot(hidden, down_w, preferred_element_type=jnp.float32)
    mixed = (scale_col * expert_out).astype(jnp.bfloat16)
    return gate_pre, up_pre, hidden, expert_out, mixed


def backward(cotan, scale_col, gate_pre, up_pre, expert_out, gate_w, up_w, down_w):
    cotan = cotan.astype(jnp.float32)
    comb_grad = jnp.sum(expert_out * cotan, axis=1)
    out_grad = (scale_col * cotan).astype(jnp.bfloat16)
    hidden_grad = contract_cols(out_grad, down_w)
    sig_gate = jax.nn.sigmoid(gate_pre)
    gate_grad = (hidden_grad * up_pre * sig_gate * (1.0 + gate_pre * (1.0 - sig_gate))).astype(
        jnp.bfloat16
    )
    up_grad = (hidden_grad * (gate_pre * sig_gate)).astype(jnp.bfloat16)
    in_grad = (contract_cols(gate_grad, gate_w) + contract_cols(up_grad, up_w)).astype(jnp.bfloat16)
    return comb_grad, out_grad, gate_grad, up_grad, in_grad


def pieces(array, count):
    size = array.shape[0] // count
    return [array[i * size : (i + 1) * size] for i in range(count)]


def on_device(sorted_rows, combine, cotangent, starts, w_gate, w_up, w_down):
    weights = (w_gate[0], w_up[0], w_down[0])
    count_rows = sorted_rows.shape[0]
    lead_count = jnp.remainder(starts[0], count_rows)
    lead_mask = jnp.arange(count_rows, dtype=jnp.int32) < lead_count
    scale = combine.astype(jnp.float32)
    zeros = jnp.zeros_like(scale)
    far_scale = shift(jnp.where(lead_mask, scale, zeros), -1)[:, None]
    far_rows = [shift(piece, -1) for piece in pieces(sorted_rows, X_CHUNKS)]
    far_cotan = [shift(piece, -1) for piece in pieces(cotangent, C_CHUNKS)]

    own_scale = jnp.where(lead_mask, zeros, scale)[:, None]
    gate_pre, up_pre, own_hidden, expert_out, own_mixed = forward(sorted_rows, own_scale, *weights)
    own_comb, own_outg, own_gateg, own_upg, own_ing = backward(
        cotangent, own_scale, gate_pre, up_pre, expert_out, *weights
    )

    ahead = [
        forward(rows, scale_col, *weights)
        for rows, scale_col in zip(far_rows, pieces(far_scale, X_CHUNKS))
    ]
    back_mixed = [shift(part[4], 1) for part in ahead]
    gate_pre, up_pre, hidden, expert_out = (
        jnp.concatenate([part[i] for part in ahead], axis=0) for i in range(4)
    )
    behind = [
        backward(*args, *weights)
        for args in zip(
            far_cotan,
            *(pieces(array, C_CHUNKS) for array in (far_scale, gate_pre, up_pre, expert_out)),
        )
    ]
    back_ing = [shift(part[4], 1) for part in behind]
    far_comb, far_outg, far_gateg, far_upg = (
        jnp.concatenate([part[i] for part in behind], axis=0) for i in range(4)
    )
    back_comb = shift(far_comb, 1)
    far_rows = jnp.concatenate(far_rows, axis=0)

    grad_gate = contract_rows(sorted_rows, own_gateg) + contract_rows(far_rows, far_gateg)
    grad_up = contract_rows(sorted_rows, own_upg) + contract_rows(far_rows, far_upg)
    grad_down = contract_rows(own_hidden, own_outg) + contract_rows(hidden, far_outg)
    lead_col = lead_mask[:, None]
    mixed = jnp.where(lead_col, jnp.concatenate(back_mixed, axis=0), own_mixed)
    comb_grad = jnp.where(lead_mask, back_comb, own_comb).astype(jnp.bfloat16)
    in_grad = jnp.where(lead_col, jnp.concatenate(back_ing, axis=0), own_ing)
    return (
        mixed,
        comb_grad,
        in_grad,
        grad_gate.astype(jnp.bfloat16)[None],
        grad_up.astype(jnp.bfloat16)[None],
        grad_down.astype(jnp.bfloat16)[None],
    )


def solution(mesh):
    in_specs = (
        P(AXES, None),
        P(AXES),
        P(AXES, None),
        P(AXES),
        P(AXES, None, None),
        P(AXES, None, None),
        P(AXES, None, None),
    )
    out_specs = (
        P(AXES, None),
        P(AXES),
        P(AXES, None),
        P(AXES, None, None),
        P(AXES, None, None),
        P(AXES, None, None),
    )
    return jax.shard_map(
        on_device, mesh=mesh, in_specs=in_specs, out_specs=out_specs, check_vma=False
    )
```

```python
import functools

import jax
import jax.numpy as jnp
from jax import lax
from jax.experimental import pallas as pl
from jax.experimental.pallas import tpu as pltpu
from jax.sharding import PartitionSpec as P

AXES = ("rows", "grp")
MESH = pl.DeviceIdType.MESH
F32 = jnp.float32
BF16 = jnp.bfloat16
X_CHUNKS = (64, 64, 64, 64)
C_CHUNKS = (64, 64, 64, 64)
HT = 256
DT = 512


def spans(sizes):
    start, out = 0, []
    for size in sizes:
        out.append((start, size))
        start += size
    return out


def dot(left, right):
    return jnp.dot(left, right, preferred_element_type=F32)


def dot_cols(left, right):
    return lax.dot_general(left, right, (((1,), (1,)), ((), ())), preferred_element_type=F32)


def dot_rows(left, right):
    return lax.dot_general(left, right, (((0,), (0,)), ((), ())), preferred_element_type=F32)


def tile(step, width):
    return pl.ds(pl.multiple_of(step * width, width), width)


def to_column(row_block):
    count = row_block.shape[1]
    return jnp.broadcast_to(row_block[0:1, :], (128, count)).T


def to_row(column, rows):
    return jnp.broadcast_to(column, (column.shape[0], 128)).T[0:rows, :]


def exchange_kernel(
    sizes,
    x_hbm, cot_hbm, own_scale, lead_scale, wg_hbm, wu_hbm, wd_hbm,
    own_mixed_o, own_ing_o, back_mixed_o, back_ing_o, own_comb_o, back_comb_o,
    far_x_o, hid_o, gg_o, ug_o, og_o,
    wg, wu, wd, x, cot, far_x, far_cot, far_scale, own_col, far_col,
    gate, up, far_gate, far_up, far_out, hid, gg, ug, og,
    own_mixed, own_ing, send_mixed, send_ing, far_comb, comb_row,
    load_sem, store_sem, scale_sem, x_sem, c_sem, m_sem, i_sem, comb_sem,
):
    n_rows, n_grp = sizes
    count = x.shape[0]
    d_tiles, h_tiles = x.shape[1] // DT, gate.shape[1] // HT
    row, col = lax.axis_index("rows"), lax.axis_index("grp")
    me = row * n_grp + col
    left = lax.rem(me + n_rows * n_grp - 1, n_rows * n_grp)
    right = lax.rem(me + 1, n_rows * n_grp)
    left_id = (left // n_grp, lax.rem(left, n_grp))
    right_id = (right // n_grp, lax.rem(right, n_grp))

    loads = [
        pltpu.make_async_copy(src, dst, load_sem.at[i])
        for i, (src, dst) in enumerate(
            ((wg_hbm, wg), (wu_hbm, wu), (wd_hbm, wd), (x_hbm, x), (cot_hbm, cot))
        )
    ]
    for load in loads:
        load.start()

    barrier = pltpu.get_barrier_semaphore()
    for peer in (left_id, right_id):
        pl.semaphore_signal(barrier, inc=1, device_id=peer, device_id_type=MESH)
    pl.semaphore_wait(barrier, 2)

    def remote(src, dst, sems, index, peer):
        return pltpu.make_async_remote_copy(
            src_ref=src,
            dst_ref=dst,
            send_sem=sems.at[0, index],
            recv_sem=sems.at[1, index],
            device_id=peer,
            device_id_type=MESH,
        )

    scale_copy = remote(lead_scale, far_scale, scale_sem, 0, left_id)
    scale_copy.start()
    x_copies, c_copies = [], []
    for i, (lo, size) in enumerate(spans(X_CHUNKS)):
        at = pl.ds(lo, size)
        x_copies.append(remote(x_hbm.at[at], far_x.at[at], x_sem, i, left_id))
        x_copies[-1].start()
    for i, (lo, size) in enumerate(spans(C_CHUNKS)):
        at = pl.ds(lo, size)
        c_copies.append(remote(cot_hbm.at[at], far_cot.at[at], c_sem, i, left_id))
        c_copies[-1].start()

    own_col[...] = to_column(own_scale[...])
    scale_copy.wait()
    far_col[...] = to_column(far_scale[...])
    loads[0].wait()
    loads[1].wait()
    loads[2].wait()

    def gate_up(rows_ref, at, gate_ref, up_ref, hid_at):
        @pl.loop(0, h_tiles)
        def _(step):
            cols = tile(step, HT)
            rows = rows_ref[at, :]
            g = dot(rows, wg[:, cols])
            u = dot(rows, wu[:, cols])
            gate_ref[at, cols] = g
            up_ref[at, cols] = u
            hid[hid_at, cols] = (g * jax.nn.sigmoid(g) * u).astype(BF16)

    def hidden_grads(og_at, act_at, gate_ref, up_ref):
        @pl.loop(0, h_tiles)
        def _(step):
            cols = tile(step, HT)
            hg = dot_cols(og[og_at, :], wd[cols, :])
            g, u = gate_ref[act_at, cols], up_ref[act_at, cols]
            s = jax.nn.sigmoid(g)
            gg[og_at, cols] = (hg * u * s * (1.0 + g * (1.0 - s))).astype(BF16)
            ug[og_at, cols] = (hg * (g * s)).astype(BF16)

    def input_grads(og_at, out_ref, out_at):
        @pl.loop(0, d_tiles)
        def _(step):
            cols = tile(step, DT)
            total = dot_cols(gg[og_at, :], wg[cols, :]) + dot_cols(ug[og_at, :], wu[cols, :])
            out_ref[out_at, cols] = total.astype(BF16)

    def far_forward(lo, size):
        at, hid_at = pl.ds(lo, size), pl.ds(count + lo, size)
        gate_up(far_x, at, far_gate, far_up, hid_at)

        @pl.loop(0, d_tiles)
        def _(step):
            cols = tile(step, DT)
            out = dot(hid[hid_at, :], wd[:, cols])
            far_out[at, cols] = out
            send_mixed[at, cols] = (far_col[at, 0:1] * out).astype(BF16)

    def far_backward(lo, size):
        at, og_at = pl.ds(lo, size), pl.ds(count + lo, size)

        def body(step, total):
            cols = tile(step, DT)
            c = far_cot[at, cols].astype(F32)
            og[og_at, cols] = (far_col[at, 0:1] * c).astype(BF16)
            return total + jnp.sum(far_out[at, cols] * c, axis=1, keepdims=True)

        total = lax.fori_loop(0, d_tiles, body, jnp.zeros((size, 1), F32))
        far_comb[at, :] = jnp.broadcast_to(total, (size, 128))
        hidden_grads(og_at, at, far_gate, far_up)
        input_grads(og_at, send_ing, at)

    own = pl.ds(0, count)

    def own_gate_up():
        loads[3].wait()
        gate_up(x, own, gate, up, own)

    def own_down():
        loads[4].wait()

        def body(step, total):
            cols = tile(step, DT)
            out = dot(hid[own, :], wd[:, cols])
            own_mixed[:, cols] = (own_col[:, 0:1] * out).astype(BF16)
            c = cot[:, cols].astype(F32)
            og[own, cols] = (own_col[:, 0:1] * c).astype(BF16)
            return total + jnp.sum(out * c, axis=1, keepdims=True)

        total = lax.fori_loop(0, d_tiles, body, jnp.zeros((count, 1), F32))
        own_comb_o[...] = to_row(total, own_comb_o.shape[0])

    stores = []

    def store(src, dst):
        stores.append(pltpu.make_async_copy(src, dst, store_sem.at[len(stores)]))
        stores[-1].start()

    def own_hidden_grads():
        store(own_mixed, own_mixed_o)
        hidden_grads(own, own, gate, up)

    def own_input_grads():
        input_grads(own, own_ing, own)
        store(own_ing, own_ing_o)

    own_steps = [own_gate_up, own_down, own_hidden_grads, own_input_grads]
    m_copies, i_copies = [], []
    for i, (lo, size) in enumerate(spans(X_CHUNKS)):
        x_copies[i].wait_recv()
        far_forward(lo, size)
        at = pl.ds(lo, size)
        m_copies.append(remote(send_mixed.at[at], back_mixed_o.at[at], m_sem, i, right_id))
        m_copies[-1].start()
        if own_steps:
            own_steps.pop(0)()
    store(far_x, far_x_o)
    store(hid, hid_o)
    for i, (lo, size) in enumerate(spans(C_CHUNKS)):
        c_copies[i].wait_recv()
        far_backward(lo, size)
        at = pl.ds(lo, size)
        i_copies.append(remote(send_ing.at[at], back_ing_o.at[at], i_sem, i, right_id))
        i_copies[-1].start()
        if own_steps:
            own_steps.pop(0)()
    for src, dst in ((gg, gg_o), (ug, ug_o), (og, og_o)):
        store(src, dst)
    comb_row[...] = far_comb[...].T[0 : comb_row.shape[0], :]
    comb_copy = remote(comb_row, back_comb_o, comb_sem, 0, right_id)
    comb_copy.start()
    for copy in stores:
        copy.wait()
    for copy in x_copies + c_copies:
        copy.wait_send()
    for copy in m_copies + i_copies:
        copy.wait()
    comb_copy.wait()


def exchange(sizes, x, cot, own_scale, lead_scale, wg, wu, wd):
    count, d = x.shape
    h = wg.shape[1]
    big = jax.ShapeDtypeStruct((count, d), BF16)
    small = jax.ShapeDtypeStruct((8, count), F32)
    act = jax.ShapeDtypeStruct((2 * count, h), BF16)
    anywhere = pl.BlockSpec(memory_space=pl.ANY)
    vmem = pl.BlockSpec(memory_space=pltpu.VMEM)
    dma = pltpu.SemaphoreType.DMA
    return pl.pallas_call(
        functools.partial(exchange_kernel, sizes),
        name="exchange",
        out_shape=(big, big, big, big, small, small, big, act, act, act,
                   jax.ShapeDtypeStruct((2 * count, d), BF16)),
        in_specs=[anywhere, anywhere, vmem, vmem, anywhere, anywhere, anywhere],
        out_specs=(anywhere,) * 4 + (vmem, anywhere) + (anywhere,) * 5,
        scratch_shapes=[
            pltpu.VMEM((d, h), BF16),
            pltpu.VMEM((d, h), BF16),
            pltpu.VMEM((h, d), BF16),
            pltpu.VMEM((count, d), BF16),
            pltpu.VMEM((count, d), BF16),
            pltpu.VMEM((count, d), BF16),
            pltpu.VMEM((count, d), BF16),
            pltpu.VMEM((8, count), F32),
            pltpu.VMEM((count, 128), F32),
            pltpu.VMEM((count, 128), F32),
            pltpu.VMEM((count, h), F32),
            pltpu.VMEM((count, h), F32),
            pltpu.VMEM((count, h), F32),
            pltpu.VMEM((count, h), F32),
            pltpu.VMEM((count, d), F32),
            pltpu.VMEM((2 * count, h), BF16),
            pltpu.VMEM((2 * count, h), BF16),
            pltpu.VMEM((2 * count, h), BF16),
            pltpu.VMEM((2 * count, d), BF16),
            pltpu.VMEM((count, d), BF16),
            pltpu.VMEM((count, d), BF16),
            pltpu.VMEM((count, d), BF16),
            pltpu.VMEM((count, d), BF16),
            pltpu.VMEM((count, 128), F32),
            pltpu.VMEM((8, count), F32),
            dma((5,)),
            dma((7,)),
            dma((2, 1)),
            dma((2, len(X_CHUNKS))),
            dma((2, len(C_CHUNKS))),
            dma((2, len(X_CHUNKS))),
            dma((2, len(C_CHUNKS))),
            dma((2, 1)),
        ],
        compiler_params=pltpu.CompilerParams(
            collective_id=0, has_side_effects=True, vmem_limit_bytes=48 * 2**20
        ),
    )(x, cot, own_scale, lead_scale, wg, wu, wd)


def finish_kernel(
    lead_ref, x, far_x, hid, gg, ug, og, own_mixed, own_ing, back_mixed, back_ing,
    grad_gate, grad_up, grad_down, mixed, ing,
):
    count = x.shape[0]
    own, far = pl.ds(0, count), pl.ds(count, count)
    grad_gate[0] = (dot_rows(x[...], gg[own, :]) + dot_rows(far_x[...], gg[far, :])).astype(BF16)
    grad_up[0] = (dot_rows(x[...], ug[own, :]) + dot_rows(far_x[...], ug[far, :])).astype(BF16)
    grad_down[0] = dot_rows(hid[...], og[...]).astype(BF16)
    lead = lax.broadcasted_iota(jnp.int32, mixed.shape, 0) < lead_ref[0]
    mixed[...] = jnp.where(lead, back_mixed[...], own_mixed[...])
    ing[...] = jnp.where(lead, back_ing[...], own_ing[...])


def finish(lead_count, x, far_x, hid, gg, ug, og, own_mixed, own_ing, back_mixed, back_ing):
    count, d = x.shape
    h = hid.shape[1]
    width = 256
    cols = pl.BlockSpec((count, width), lambda i, lead: (0, i))
    both = pl.BlockSpec((2 * count, width), lambda i, lead: (0, i))
    act = pl.BlockSpec((2 * count, h), lambda i, lead: (0, 0))
    tall = pl.BlockSpec((1, width, h), lambda i, lead: (0, i, 0))
    wide = pl.BlockSpec((1, h, width), lambda i, lead: (0, 0, i))
    return pl.pallas_call(
        finish_kernel,
        name="finish",
        out_shape=(
            jax.ShapeDtypeStruct((1, d, h), BF16),
            jax.ShapeDtypeStruct((1, d, h), BF16),
            jax.ShapeDtypeStruct((1, h, d), BF16),
            jax.ShapeDtypeStruct((count, d), BF16),
            jax.ShapeDtypeStruct((count, d), BF16),
        ),
        grid_spec=pltpu.PrefetchScalarGridSpec(
            num_scalar_prefetch=1,
            grid=(d // width,),
            in_specs=[cols, cols, act, act, act, both, cols, cols, cols, cols],
            out_specs=(tall, tall, wide, cols, cols),
        ),
        compiler_params=pltpu.CompilerParams(vmem_limit_bytes=32 * 2**20),
    )(lead_count, x, far_x, hid, gg, ug, og, own_mixed, own_ing, back_mixed, back_ing)


def solution(mesh):
    sizes = tuple(mesh.shape[axis] for axis in AXES)

    def on_device(sorted_rows, combine, cotangent, starts, w_gate, w_up, w_down):
        count = sorted_rows.shape[0]
        lead_count = jnp.remainder(starts, count)
        lead = jnp.arange(count, dtype=jnp.int32) < lead_count[0]
        scale = combine.astype(F32)
        zeros = jnp.zeros_like(scale)
        own_scale = jnp.broadcast_to(jnp.where(lead, zeros, scale), (8, count))
        lead_scale = jnp.broadcast_to(jnp.where(lead, scale, zeros), (8, count))
        (own_mixed, own_ing, back_mixed, back_ing, own_comb, back_comb, far_x, hid, gg, ug, og) = exchange(
            sizes, sorted_rows, cotangent, own_scale, lead_scale, w_gate[0], w_up[0], w_down[0]
        )
        grad_gate, grad_up, grad_down, mixed, ing = finish(
            lead_count, sorted_rows, far_x, hid, gg, ug, og, own_mixed, own_ing, back_mixed, back_ing
        )
        comb_grad = jnp.where(lead, back_comb[0], own_comb[0]).astype(BF16)
        return mixed, comb_grad, ing, grad_gate, grad_up, grad_down

    rows2, rows1, rows3 = P(AXES, None), P(AXES), P(AXES, None, None)
    return jax.shard_map(
        on_device,
        mesh=mesh,
        in_specs=(rows2, rows1, rows2, rows1, rows3, rows3, rows3),
        out_specs=(rows2, rows1, rows2, rows3, rows3, rows3),
        check_vma=False,
    )
```

```python
import functools

import jax
import jax.numpy as jnp
from jax import lax
from jax.experimental import pallas as pl
from jax.experimental.pallas import tpu as pltpu
from jax.sharding import PartitionSpec as P

AXES = ("rows", "grp")
MESH = pl.DeviceIdType.MESH
F32 = jnp.float32
BF16 = jnp.bfloat16
X_CHUNKS = (32, 32, 64, 64, 64)
C_CHUNKS = (64, 64, 64, 32, 32)
HT = 256
DT = 512


def spans(sizes):
    start, out = 0, []
    for size in sizes:
        out.append((start, size))
        start += size
    return out


def dot(left, right):
    return jnp.dot(left, right, preferred_element_type=F32)


def dot_cols(left, right):
    return lax.dot_general(left, right, (((1,), (1,)), ((), ())), preferred_element_type=F32)


def dot_rows(left, right):
    return lax.dot_general(left, right, (((0,), (0,)), ((), ())), preferred_element_type=F32)


def tiles(extent, width):
    return [pl.ds(lo, width) for lo in range(0, extent, width)]


def to_column(row):
    return jnp.broadcast_to(row, (128, row.shape[1])).T


def exchange_kernel(
    sizes,
    starts, combine, x_hbm, cot_hbm, wg_hbm, wu_hbm, wd_hbm,
    mixed, ing, comb, grad_gate, grad_up, grad_down,
    wg, wu, wd, x, cot, scale_out, scale_in, own_col, far_col,
    gate, up, far_gate, far_up, far_out, hid, gg, ug, og,
    send_mixed, send_ing, back_mixed, back_ing, own_comb, far_comb, comb_out, comb_in,
    load_sem, scale_sem, x_sem, c_sem, m_sem, i_sem, comb_sem,
):
    n_rows, n_grp = sizes
    last = n_rows * n_grp - 1
    count, d = x_hbm.shape
    h = gate.shape[1]
    own, far = pl.ds(0, count), pl.ds(count, count)
    me = lax.axis_index("rows") * n_grp + lax.axis_index("grp")
    has_left, has_right = me > 0, me < last
    left = lax.rem(me + last, last + 1)
    right = lax.rem(me + 1, last + 1)
    left_id = (left // n_grp, lax.rem(left, n_grp))
    right_id = (right // n_grp, lax.rem(right, n_grp))

    loads = [
        pltpu.make_async_copy(src, dst, load_sem.at[i])
        for i, (src, dst) in enumerate(
            (
                (wg_hbm, wg),
                (wu_hbm, wu),
                (wd_hbm, wd),
                (x_hbm, x.at[own]),
                (cot_hbm, cot.at[own]),
            )
        )
    ]
    for load in loads:
        load.start()

    barrier = pltpu.get_barrier_semaphore()

    @pl.when(has_left)
    def _():
        pl.semaphore_signal(barrier, inc=1, device_id=left_id, device_id_type=MESH)

    @pl.when(has_right)
    def _():
        pl.semaphore_signal(barrier, inc=1, device_id=right_id, device_id_type=MESH)

    lead_count = lax.rem(starts[0], count)
    row_lead = lax.broadcasted_iota(jnp.int32, (1, count), 1) < lead_count
    scale = combine[...].astype(F32).reshape(1, count)
    zero_row = jnp.zeros_like(scale)
    scale_out[...] = jnp.broadcast_to(jnp.where(row_lead, scale, zero_row), scale_out.shape)
    own_col[...] = to_column(jnp.where(row_lead, zero_row, scale))

    @pl.when(has_left & has_right)
    def _():
        pl.semaphore_wait(barrier, 2)

    @pl.when(jnp.logical_not(has_left & has_right))
    def _():
        pl.semaphore_wait(barrier, 1)

    def remote(src, dst, sems, index, peer):
        return pltpu.make_async_remote_copy(
            src_ref=src,
            dst_ref=dst,
            send_sem=sems.at[0, index],
            recv_sem=sems.at[1, index],
            device_id=peer,
            device_id_type=MESH,
        )

    scale_copy = remote(scale_out, scale_in, scale_sem, 0, left_id)
    x_copies = [
        remote(x_hbm.at[pl.ds(lo, size)], x.at[pl.ds(count + lo, size)], x_sem, i, left_id)
        for i, (lo, size) in enumerate(spans(X_CHUNKS))
    ]
    c_copies = [
        remote(cot_hbm.at[pl.ds(lo, size)], cot.at[pl.ds(count + lo, size)], c_sem, i, left_id)
        for i, (lo, size) in enumerate(spans(C_CHUNKS))
    ]
    m_copies = [
        remote(send_mixed.at[pl.ds(lo, size)], back_mixed.at[pl.ds(lo, size)], m_sem, i, right_id)
        for i, (lo, size) in enumerate(spans(X_CHUNKS))
    ]
    i_copies = [
        remote(send_ing.at[pl.ds(lo, size)], back_ing.at[pl.ds(lo, size)], i_sem, i, right_id)
        for i, (lo, size) in enumerate(spans(C_CHUNKS))
    ]
    comb_copy = remote(comb_out, comb_in, comb_sem, 0, right_id)

    @pl.when(has_left)
    def _():
        scale_copy.start()
        for copy in x_copies + c_copies:
            copy.start()

    @pl.when(jnp.logical_not(has_right))
    def _():
        scale_in[...] = jnp.zeros_like(scale_in)
        x[far, :] = jnp.zeros((count, d), BF16)
        cot[far, :] = jnp.zeros((count, d), BF16)

    @pl.when(jnp.logical_not(has_left))
    def _():
        comb_in[...] = jnp.zeros_like(comb_in)
        back_mixed[...] = jnp.zeros_like(back_mixed)
        back_ing[...] = jnp.zeros_like(back_ing)

    def arrive(copy):
        pl.when(has_right)(copy.wait_recv)

    def send_back(copy):
        pl.when(has_right)(copy.start)

    loads[0].wait()
    loads[1].wait()

    def gate_up(at, gate_ref, up_ref, act_at):
        for cols in tiles(h, HT):
            rows = x[at, :]
            g = dot(rows, wg[:, cols])
            u = dot(rows, wu[:, cols])
            gate_ref[act_at, cols] = g
            up_ref[act_at, cols] = u
            hid[at, cols] = (g * jax.nn.sigmoid(g) * u).astype(BF16)

    def hidden_grads(at, act_at, gate_ref, up_ref):
        for cols in tiles(h, HT):
            hg = dot_cols(og[at, :], wd[cols, :])
            g, u = gate_ref[act_at, cols], up_ref[act_at, cols]
            s = jax.nn.sigmoid(g)
            gg[at, cols] = (hg * u * s * (1.0 + g * (1.0 - s))).astype(BF16)
            ug[at, cols] = (hg * (g * s)).astype(BF16)

    def input_grads(at, out_ref, out_at):
        for cols in tiles(d, DT):
            total = dot_cols(gg[at, :], wg[cols, :]) + dot_cols(ug[at, :], wu[cols, :])
            out_ref[out_at, cols] = total.astype(BF16)

    def far_forward(lo, size):
        at, act_at = pl.ds(count + lo, size), pl.ds(lo, size)
        gate_up(at, far_gate, far_up, act_at)
        for cols in tiles(d, DT):
            out = dot(hid[at, :], wd[:, cols])
            far_out[act_at, cols] = out
            send_mixed[act_at, cols] = (far_col[act_at, 0:1] * out).astype(BF16)

    def far_backward(lo, size):
        at, act_at = pl.ds(count + lo, size), pl.ds(lo, size)
        total = jnp.zeros((size, 1), F32)
        for cols in tiles(d, DT):
            c = cot[at, cols].astype(F32)
            og[at, cols] = (far_col[act_at, 0:1] * c).astype(BF16)
            total = total + jnp.sum(far_out[act_at, cols] * c, axis=1, keepdims=True)
        far_comb[act_at, :] = jnp.broadcast_to(total, (size, 128))
        hidden_grads(at, act_at, far_gate, far_up)
        input_grads(at, send_ing, act_at)

    def own_forward():
        loads[3].wait()
        gate_up(own, gate, up, own)

    def own_down():
        loads[4].wait()
        total = jnp.zeros((count, 1), F32)
        for cols in tiles(d, DT):
            out = dot(hid[own, :], wd[:, cols])
            mixed[:, cols] = (own_col[:, 0:1] * out).astype(BF16)
            c = cot[own, cols].astype(F32)
            og[own, cols] = (own_col[:, 0:1] * c).astype(BF16)
            total = total + jnp.sum(out * c, axis=1, keepdims=True)
        own_comb[...] = jnp.broadcast_to(total, (count, 128))

    def own_hidden_grads():
        hidden_grads(own, own, gate, up)

    def own_input_grads():
        input_grads(own, ing, own)

    arrive(scale_copy)
    far_col[...] = to_column(scale_in[0:1, :])
    own_steps = [own_forward, own_down, own_hidden_grads, own_input_grads]
    for i, (lo, size) in enumerate(spans(X_CHUNKS)):
        arrive(x_copies[i])
        if i == 0:
            loads[2].wait()
        far_forward(lo, size)
        send_back(m_copies[i])
        if i > 0 and own_steps:
            own_steps.pop(0)()
    for i, (lo, size) in enumerate(spans(C_CHUNKS)):
        arrive(c_copies[i])
        far_backward(lo, size)
        send_back(i_copies[i])
        if own_steps:
            own_steps.pop(0)()
    comb_out[...] = far_comb[...].T[0 : comb_out.shape[0], :]
    send_back(comb_copy)

    for cols in tiles(d, DT):
        rows = x[:, cols]
        grad_gate[cols, :] = dot_rows(rows, gg[...]).astype(BF16)
        grad_up[cols, :] = dot_rows(rows, ug[...]).astype(BF16)
    for cols in tiles(d, DT):
        grad_down[:, cols] = dot_rows(hid[...], og[:, cols]).astype(BF16)

    def select(back, out, lo, size):
        at = pl.ds(lo, size)
        lead = lax.broadcasted_iota(jnp.int32, (size, d), 0) + lo < lead_count
        out[at, :] = jnp.where(lead, back[at, :], out[at, :])

    for copies, back, out, sizes_ in (
        (m_copies, back_mixed, mixed, X_CHUNKS),
        (i_copies, back_ing, ing, C_CHUNKS),
    ):
        for copy, (lo, size) in zip(copies, spans(sizes_)):
            pl.when(has_left)(copy.wait_recv)
            select(back, out, lo, size)
    pl.when(has_left)(comb_copy.wait_recv)
    comb[...] = jnp.where(
        jnp.broadcast_to(row_lead, comb.shape), comb_in[...], own_comb[...].T[0 : comb.shape[0], :]
    )

    @pl.when(has_left)
    def _():
        for copy in [scale_copy] + x_copies + c_copies:
            copy.wait_send()

    @pl.when(has_right)
    def _():
        for copy in m_copies + i_copies + [comb_copy]:
            copy.wait_send()


def exchange(sizes, starts, combine, x, cot, wg, wu, wd):
    count, d = x.shape
    h = wg.shape[1]
    anywhere = pl.BlockSpec(memory_space=pl.ANY)
    vmem = pl.BlockSpec(memory_space=pltpu.VMEM)
    smem = pl.BlockSpec(memory_space=pltpu.SMEM)
    dma = pltpu.SemaphoreType.DMA
    return pl.pallas_call(
        functools.partial(exchange_kernel, sizes),
        name="exchange",
        out_shape=(
            jax.ShapeDtypeStruct((count, d), BF16),
            jax.ShapeDtypeStruct((count, d), BF16),
            jax.ShapeDtypeStruct((8, count), F32),
            jax.ShapeDtypeStruct((d, h), BF16),
            jax.ShapeDtypeStruct((d, h), BF16),
            jax.ShapeDtypeStruct((h, d), BF16),
        ),
        in_specs=[smem, vmem] + [pl.BlockSpec(memory_space=pltpu.HBM)] * 5,
        out_specs=(vmem,) * 6,
        scratch_shapes=[
            pltpu.VMEM((d, h), BF16),
            pltpu.VMEM((d, h), BF16),
            pltpu.VMEM((h, d), BF16),
            pltpu.VMEM((2 * count, d), BF16),
            pltpu.VMEM((2 * count, d), BF16),
            pltpu.VMEM((8, count), F32),
            pltpu.VMEM((8, count), F32),
            pltpu.VMEM((count, 128), F32),
            pltpu.VMEM((count, 128), F32),
            pltpu.VMEM((count, h), F32),
            pltpu.VMEM((count, h), F32),
            pltpu.VMEM((count, h), F32),
            pltpu.VMEM((count, h), F32),
            pltpu.VMEM((count, d), F32),
            pltpu.VMEM((2 * count, h), BF16),
            pltpu.VMEM((2 * count, h), BF16),
            pltpu.VMEM((2 * count, h), BF16),
            pltpu.VMEM((2 * count, d), BF16),
            pltpu.VMEM((count, d), BF16),
            pltpu.VMEM((count, d), BF16),
            pltpu.VMEM((count, d), BF16),
            pltpu.VMEM((count, d), BF16),
            pltpu.VMEM((count, 128), F32),
            pltpu.VMEM((count, 128), F32),
            pltpu.VMEM((8, count), F32),
            pltpu.VMEM((8, count), F32),
            dma((5,)),
            dma((2, 1)),
            dma((2, len(X_CHUNKS))),
            dma((2, len(C_CHUNKS))),
            dma((2, len(X_CHUNKS))),
            dma((2, len(C_CHUNKS))),
            dma((2, 1)),
        ],
        compiler_params=pltpu.CompilerParams(
            collective_id=0, has_side_effects=True, vmem_limit_bytes=30 * 2**20
        ),
    )(starts, combine, *(pltpu.with_memory_space_constraint(a, pltpu.HBM) for a in (x, cot, wg, wu, wd)))


def finish_kernel(mixed, ing, comb, gate, up, down, mixed_o, ing_o, comb_o, gate_o, up_o, down_o, sem):
    copies = [
        pltpu.make_async_copy(src, dst, sem.at[i])
        for i, (src, dst) in enumerate(
            ((gate, gate_o.at[0]), (up, up_o.at[0]), (down, down_o.at[0]), (mixed, mixed_o), (ing, ing_o))
        )
    ]
    for copy in copies:
        copy.start()
    comb_o[...] = comb[0:1, :].reshape(comb_o.shape).astype(BF16)
    for copy in copies:
        copy.wait()


def finish(mixed, ing, comb, gate, up, down):
    anywhere = pl.BlockSpec(memory_space=pl.ANY)
    vmem = pl.BlockSpec(memory_space=pltpu.VMEM)
    return pl.pallas_call(
        finish_kernel,
        name="finish",
        out_shape=(
            jax.ShapeDtypeStruct(mixed.shape, BF16),
            jax.ShapeDtypeStruct(ing.shape, BF16),
            jax.ShapeDtypeStruct(comb.shape[1:], BF16),
            jax.ShapeDtypeStruct((1,) + gate.shape, BF16),
            jax.ShapeDtypeStruct((1,) + up.shape, BF16),
            jax.ShapeDtypeStruct((1,) + down.shape, BF16),
        ),
        in_specs=[vmem] * 6,
        out_specs=(anywhere, anywhere, vmem) + (anywhere,) * 3,
        scratch_shapes=[pltpu.SemaphoreType.DMA((5,))],
        compiler_params=pltpu.CompilerParams(vmem_limit_bytes=2 * 2**20),
    )(*(pltpu.with_memory_space_constraint(a, pltpu.VMEM) for a in (mixed, ing, comb, gate, up, down)))


def solution(mesh):
    sizes = tuple(mesh.shape[axis] for axis in AXES)

    def on_device(sorted_rows, combine, cotangent, starts, w_gate, w_up, w_down):
        mixed, ing, comb, gate, up, down = exchange(
            sizes, starts, combine, sorted_rows, cotangent, w_gate[0], w_up[0], w_down[0]
        )
        mixed, ing, comb, gate, up, down = finish(mixed, ing, comb, gate, up, down)
        return mixed, comb, ing, gate, up, down

    rows2, rows1, rows3 = P(AXES, None), P(AXES), P(AXES, None, None)
    return jax.shard_map(
        on_device,
        mesh=mesh,
        in_specs=(rows2, rows1, rows2, rows1, rows3, rows3, rows3),
        out_specs=(rows2, rows1, rows2, rows3, rows3, rows3),
        check_vma=False,
    )
```

```python
import functools

import jax
import jax.numpy as jnp
from jax import lax
from jax.experimental import pallas as pl
from jax.experimental.pallas import tpu as pltpu
from jax.sharding import PartitionSpec as P

AXES = ("rows", "grp")
MESH = pl.DeviceIdType.MESH
F32 = jnp.float32
BF16 = jnp.bfloat16
CHUNK = 32
HT = 256
DT = 512


def dot(left, right):
    return jnp.dot(left, right, preferred_element_type=F32)


def dot_rows(left, right):
    return lax.dot_general(left, right, (((0,), (0,)), ((), ())), preferred_element_type=F32)


def tiles(extent, width):
    return [pl.ds(lo, width) for lo in range(0, extent, width)]


def to_column(row):
    return jnp.broadcast_to(row, (128, row.shape[1])).T


def exchange_kernel(
    sizes,
    starts, combine, x_hbm, cot_hbm, wg_hbm, wu_hbm, wd_hbm,
    mixed, ing, comb, grad_gate, grad_up, grad_down,
    wg, wu, wd, wg_t, wu_t, wd_t, x, cot, scale_out, scale_in, own_col, far_col,
    gate, up, far_gate, far_up, far_out, hid, gg, ug, og,
    send_mixed, send_ing, back_mixed, back_ing, own_comb, far_comb, comb_out, comb_in,
    load_sem, scale_sem, x_sem, c_sem, m_sem, i_sem, comb_sem,
):
    n_rows, n_grp = sizes
    last = n_rows * n_grp - 1
    count, d = x_hbm.shape
    h = gate.shape[1]
    own, far = pl.ds(0, count), pl.ds(count, count)
    me = lax.axis_index("rows") * n_grp + lax.axis_index("grp")
    has_left, has_right = me > 0, me < last
    left = lax.rem(me + last, last + 1)
    right = lax.rem(me + 1, last + 1)
    left_id = (left // n_grp, lax.rem(left, n_grp))
    right_id = (right // n_grp, lax.rem(right, n_grp))

    loads = [
        pltpu.make_async_copy(src, dst, load_sem.at[i])
        for i, (src, dst) in enumerate(
            (
                (wg_hbm, wg),
                (wu_hbm, wu),
                (wd_hbm, wd),
                (x_hbm, x.at[own]),
                (cot_hbm, cot.at[own]),
            )
        )
    ]
    for load in loads:
        load.start()

    barrier = pltpu.get_barrier_semaphore()

    @pl.when(has_left)
    def _():
        pl.semaphore_signal(barrier, inc=1, device_id=left_id, device_id_type=MESH)

    @pl.when(has_right)
    def _():
        pl.semaphore_signal(barrier, inc=1, device_id=right_id, device_id_type=MESH)

    lead_count = lax.rem(starts[0], count)
    row_lead = lax.broadcasted_iota(jnp.int32, (1, count), 1) < lead_count
    scale = combine[...].astype(F32).reshape(1, count)
    zero_row = jnp.zeros_like(scale)
    scale_out[...] = jnp.broadcast_to(jnp.where(row_lead, scale, zero_row), scale_out.shape)
    own_col[...] = to_column(jnp.where(row_lead, zero_row, scale))

    @pl.when(has_left & has_right)
    def _():
        pl.semaphore_wait(barrier, 2)

    @pl.when(jnp.logical_not(has_left & has_right))
    def _():
        pl.semaphore_wait(barrier, 1)

    def remote(src, dst, sems, index, peer):
        return pltpu.make_async_remote_copy(
            src_ref=src,
            dst_ref=dst,
            send_sem=sems.at[0, index],
            recv_sem=sems.at[1, index],
            device_id=peer,
            device_id_type=MESH,
        )

    scale_copy = remote(scale_out, scale_in, scale_sem, 0, left_id)
    pieces = count // CHUNK

    def piece(i, base=0):
        return pl.ds(pl.multiple_of(base + i * CHUNK, CHUNK), CHUNK)

    def x_copy(i):
        return remote(x_hbm.at[piece(i)], x.at[piece(i, count)], x_sem, i, left_id)

    def c_copy(i):
        return remote(cot_hbm.at[piece(i)], cot.at[piece(i, count)], c_sem, i, left_id)

    def m_copy(i):
        return remote(send_mixed.at[piece(i)], back_mixed.at[piece(i)], m_sem, i, right_id)

    def i_copy(i):
        return remote(send_ing.at[piece(i)], back_ing.at[piece(i)], i_sem, i, right_id)

    comb_copy = remote(comb_out, comb_in, comb_sem, 0, right_id)

    @pl.when(has_left)
    def _():
        scale_copy.start()
        for i in range(pieces):
            x_copy(i).start()
        for i in range(pieces):
            c_copy(i).start()

    @pl.when(jnp.logical_not(has_right))
    def _():
        scale_in[...] = jnp.zeros_like(scale_in)
        x[far, :] = jnp.zeros((count, d), BF16)
        cot[far, :] = jnp.zeros((count, d), BF16)

    @pl.when(jnp.logical_not(has_left))
    def _():
        comb_in[...] = jnp.zeros_like(comb_in)
        back_mixed[...] = jnp.zeros_like(back_mixed)
        back_ing[...] = jnp.zeros_like(back_ing)

    def arrive(copy):
        pl.when(has_right)(copy.wait_recv)

    def send_back(copy):
        pl.when(has_right)(copy.start)

    def gate_up(at, gate_ref, up_ref, act_at):
        for cols in tiles(h, HT):
            rows = x[at, :]
            g = dot(rows, wg[:, cols])
            u = dot(rows, wu[:, cols])
            gate_ref[act_at, cols] = g
            up_ref[act_at, cols] = u
            hid[at, cols] = (g * jax.nn.sigmoid(g) * u).astype(BF16)

    def hidden_grads(at, act_at, gate_ref, up_ref):
        for cols in tiles(h, HT):
            hg = dot(og[at, :], wd_t[:, cols])
            g, u = gate_ref[act_at, cols], up_ref[act_at, cols]
            s = jax.nn.sigmoid(g)
            gg[at, cols] = (hg * u * s * (1.0 + g * (1.0 - s))).astype(BF16)
            ug[at, cols] = (hg * (g * s)).astype(BF16)

    def input_grads(at, out_ref, out_at):
        for cols in tiles(d, DT):
            total = dot(gg[at, :], wg_t[:, cols]) + dot(ug[at, :], wu_t[:, cols])
            out_ref[out_at, cols] = total.astype(BF16)

    def far_forward(i):
        at, act_at = piece(i, count), piece(i)
        gate_up(at, far_gate, far_up, act_at)
        for cols in tiles(d, DT):
            out = dot(hid[at, :], wd[:, cols])
            far_out[act_at, cols] = out
            send_mixed[act_at, cols] = (far_col[act_at, 0:1] * out).astype(BF16)

    def far_backward(i):
        at, act_at = piece(i, count), piece(i)
        total = jnp.zeros((CHUNK, 1), F32)
        for cols in tiles(d, DT):
            c = cot[at, cols].astype(F32)
            og[at, cols] = (far_col[act_at, 0:1] * c).astype(BF16)
            total = total + jnp.sum(far_out[act_at, cols] * c, axis=1, keepdims=True)
        far_comb[act_at, :] = jnp.broadcast_to(total, (CHUNK, 128))
        hidden_grads(at, act_at, far_gate, far_up)
        input_grads(at, send_ing, act_at)

    def own_forward():
        gate_up(own, gate, up, own)

    def own_down():
        total = jnp.zeros((count, 1), F32)
        for cols in tiles(d, DT):
            out = dot(hid[own, :], wd[:, cols])
            mixed[:, cols] = (own_col[:, 0:1] * out).astype(BF16)
            c = cot[own, cols].astype(F32)
            og[own, cols] = (own_col[:, 0:1] * c).astype(BF16)
            total = total + jnp.sum(out * c, axis=1, keepdims=True)
        own_comb[...] = jnp.broadcast_to(total, (count, 128))

    def own_hidden_grads():
        hidden_grads(own, own, gate, up)

    def own_input_grads():
        input_grads(own, ing, own)

    def transpose_down():
        for cols in tiles(d, DT):
            wd_t[cols, :] = wd[:, cols].T

    loads[0].wait()
    for cols in tiles(d, DT):
        wg_t[:, cols] = wg[cols, :].T
    loads[1].wait()
    for cols in tiles(d, DT):
        wu_t[:, cols] = wu[cols, :].T
    for load in loads[2:]:
        load.wait()
    arrive(scale_copy)
    far_col[...] = to_column(scale_in[0:1, :])

    @pl.loop(0, pieces)
    def _(i):
        arrive(x_copy(i))
        far_forward(i)
        send_back(m_copy(i))
        for k, step in enumerate((own_forward, own_down, transpose_down)):
            pl.when(i == 2 * k + 1)(step)

    @pl.loop(0, pieces)
    def _(i):
        arrive(c_copy(i))
        far_backward(i)
        send_back(i_copy(i))
        for k, step in enumerate((own_hidden_grads, own_input_grads)):
            pl.when(i == 2 * k + 1)(step)

    comb_out[...] = far_comb[...].T[0 : comb_out.shape[0], :]
    send_back(comb_copy)

    for cols in tiles(d, DT):
        rows = x[:, cols]
        grad_gate[cols, :] = dot_rows(rows, gg[...]).astype(BF16)
        grad_up[cols, :] = dot_rows(rows, ug[...]).astype(BF16)
    for cols in tiles(d, DT):
        grad_down[:, cols] = dot_rows(hid[...], og[:, cols]).astype(BF16)

    def select(copy, back, out, i):
        pl.when(has_left)(copy(i).wait_recv)
        lead = lax.broadcasted_iota(jnp.int32, (CHUNK, d), 0) + i * CHUNK < lead_count
        out[piece(i), :] = jnp.where(lead, back[piece(i), :], out[piece(i), :])

    @pl.loop(0, pieces)
    def _(i):
        select(m_copy, back_mixed, mixed, i)

    @pl.loop(0, pieces)
    def _(i):
        select(i_copy, back_ing, ing, i)

    pl.when(has_left)(comb_copy.wait_recv)
    comb[...] = jnp.where(
        jnp.broadcast_to(row_lead, comb.shape), comb_in[...], own_comb[...].T[0 : comb.shape[0], :]
    )

    @pl.when(has_left)
    def _():
        scale_copy.wait_send()
        for i in range(pieces):
            x_copy(i).wait_send()
            c_copy(i).wait_send()

    @pl.when(has_right)
    def _():
        for i in range(pieces):
            m_copy(i).wait_send()
            i_copy(i).wait_send()
        comb_copy.wait_send()


def exchange(sizes, starts, combine, x, cot, wg, wu, wd):
    count, d = x.shape
    h = wg.shape[1]
    pieces = count // CHUNK
    anywhere = pl.BlockSpec(memory_space=pl.ANY)
    vmem = pl.BlockSpec(memory_space=pltpu.VMEM)
    smem = pl.BlockSpec(memory_space=pltpu.SMEM)
    dma = pltpu.SemaphoreType.DMA
    return pl.pallas_call(
        functools.partial(exchange_kernel, sizes),
        name="exchange",
        out_shape=(
            jax.ShapeDtypeStruct((count, d), BF16),
            jax.ShapeDtypeStruct((count, d), BF16),
            jax.ShapeDtypeStruct((8, count), F32),
            jax.ShapeDtypeStruct((d, h), BF16),
            jax.ShapeDtypeStruct((d, h), BF16),
            jax.ShapeDtypeStruct((h, d), BF16),
        ),
        in_specs=[smem, vmem] + [pl.BlockSpec(memory_space=pltpu.HBM)] * 5,
        out_specs=(vmem,) * 6,
        scratch_shapes=[
            pltpu.VMEM((d, h), BF16),
            pltpu.VMEM((d, h), BF16),
            pltpu.VMEM((h, d), BF16),
            pltpu.VMEM((h, d), BF16),
            pltpu.VMEM((h, d), BF16),
            pltpu.VMEM((d, h), BF16),
            pltpu.VMEM((2 * count, d), BF16),
            pltpu.VMEM((2 * count, d), BF16),
            pltpu.VMEM((8, count), F32),
            pltpu.VMEM((8, count), F32),
            pltpu.VMEM((count, 128), F32),
            pltpu.VMEM((count, 128), F32),
            pltpu.VMEM((count, h), F32),
            pltpu.VMEM((count, h), F32),
            pltpu.VMEM((count, h), F32),
            pltpu.VMEM((count, h), F32),
            pltpu.VMEM((count, d), F32),
            pltpu.VMEM((2 * count, h), BF16),
            pltpu.VMEM((2 * count, h), BF16),
            pltpu.VMEM((2 * count, h), BF16),
            pltpu.VMEM((2 * count, d), BF16),
            pltpu.VMEM((count, d), BF16),
            pltpu.VMEM((count, d), BF16),
            pltpu.VMEM((count, d), BF16),
            pltpu.VMEM((count, d), BF16),
            pltpu.VMEM((count, 128), F32),
            pltpu.VMEM((count, 128), F32),
            pltpu.VMEM((8, count), F32),
            pltpu.VMEM((8, count), F32),
            dma((5,)),
            dma((2, 1)),
            dma((2, pieces)),
            dma((2, pieces)),
            dma((2, pieces)),
            dma((2, pieces)),
            dma((2, 1)),
        ],
        compiler_params=pltpu.CompilerParams(
            collective_id=0, has_side_effects=True, vmem_limit_bytes=40 * 2**20
        ),
    )(starts, combine, *(pltpu.with_memory_space_constraint(a, pltpu.HBM) for a in (x, cot, wg, wu, wd)))


def finish_kernel(mixed, ing, comb, gate, up, down, mixed_o, ing_o, comb_o, gate_o, up_o, down_o, sem):
    copies = [
        pltpu.make_async_copy(src, dst, sem.at[i])
        for i, (src, dst) in enumerate(
            ((gate, gate_o.at[0]), (up, up_o.at[0]), (down, down_o.at[0]), (mixed, mixed_o), (ing, ing_o))
        )
    ]
    for copy in copies:
        copy.start()
    comb_o[...] = comb[0:1, :].reshape(comb_o.shape).astype(BF16)
    for copy in copies:
        copy.wait()


def finish(mixed, ing, comb, gate, up, down):
    anywhere = pl.BlockSpec(memory_space=pl.ANY)
    vmem = pl.BlockSpec(memory_space=pltpu.VMEM)
    return pl.pallas_call(
        finish_kernel,
        name="finish",
        out_shape=(
            jax.ShapeDtypeStruct(mixed.shape, BF16),
            jax.ShapeDtypeStruct(ing.shape, BF16),
            jax.ShapeDtypeStruct(comb.shape[1:], BF16),
            jax.ShapeDtypeStruct((1,) + gate.shape, BF16),
            jax.ShapeDtypeStruct((1,) + up.shape, BF16),
            jax.ShapeDtypeStruct((1,) + down.shape, BF16),
        ),
        in_specs=[vmem] * 6,
        out_specs=(anywhere, anywhere, vmem) + (anywhere,) * 3,
        scratch_shapes=[pltpu.SemaphoreType.DMA((5,))],
        compiler_params=pltpu.CompilerParams(vmem_limit_bytes=2 * 2**20),
    )(*(pltpu.with_memory_space_constraint(a, pltpu.VMEM) for a in (mixed, ing, comb, gate, up, down)))


def solution(mesh):
    sizes = tuple(mesh.shape[axis] for axis in AXES)

    def on_device(sorted_rows, combine, cotangent, starts, w_gate, w_up, w_down):
        mixed, ing, comb, gate, up, down = exchange(
            sizes, starts, combine, sorted_rows, cotangent, w_gate[0], w_up[0], w_down[0]
        )
        mixed, ing, comb, gate, up, down = finish(mixed, ing, comb, gate, up, down)
        return mixed, comb, ing, gate, up, down

    rows2, rows1, rows3 = P(AXES, None), P(AXES), P(AXES, None, None)
    return jax.shard_map(
        on_device,
        mesh=mesh,
        in_specs=(rows2, rows1, rows2, rows1, rows3, rows3, rows3),
        out_specs=(rows2, rows1, rows2, rows3, rows3, rows3),
        check_vma=False,
    )
```

```python
import functools

import jax
import jax.numpy as jnp
from jax import lax
from jax.experimental import pallas as pl
from jax.experimental.pallas import tpu as pltpu
from jax.sharding import PartitionSpec as P

AXES = ("rows", "grp")
MESH = pl.DeviceIdType.MESH
F32 = jnp.float32
BF16 = jnp.bfloat16
CHUNK = 32
HT = 256
DT = 512


def dot(left, right):
    return jnp.dot(left, right, preferred_element_type=F32)


def dot_rows(left, right):
    return lax.dot_general(left, right, (((0,), (0,)), ((), ())), preferred_element_type=F32)


def tiles(extent, width):
    return [pl.ds(lo, width) for lo in range(0, extent, width)]


def to_column(row):
    return jnp.broadcast_to(row, (128, row.shape[1])).T


def exchange_kernel(
    sizes,
    starts, combine, x_hbm, cot_hbm, wg_hbm, wu_hbm, wd_hbm,
    mixed, ing, comb, grad_gate, grad_up, grad_down,
    wg, wu, wd, wg_t, wu_t, wd_t, x, cot, scale_out, scale_in, own_col, far_col,
    gate, up, far_gate, far_up, far_out, hid, gg, ug, og,
    send_mixed, send_ing, back_mixed, back_ing, own_comb, far_comb, comb_out, comb_in,
    starts_s, combine_v, load_sem, scale_sem, x_sem, c_sem, m_sem, i_sem, comb_sem,
):
    n_rows, n_grp = sizes
    last = n_rows * n_grp - 1
    count, d = x_hbm.shape
    h = gate.shape[1]
    own, far = pl.ds(0, count), pl.ds(count, count)
    me = lax.axis_index("rows") * n_grp + lax.axis_index("grp")
    has_left, has_right = me > 0, me < last
    left = lax.rem(me + last, last + 1)
    right = lax.rem(me + 1, last + 1)
    left_id = (left // n_grp, lax.rem(left, n_grp))
    right_id = (right // n_grp, lax.rem(right, n_grp))

    small = [
        pltpu.make_async_copy(starts, starts_s, load_sem.at[5]),
        pltpu.make_async_copy(combine, combine_v, load_sem.at[6]),
    ]
    for load in small:
        load.start()
    loads = [
        pltpu.make_async_copy(src, dst, load_sem.at[i])
        for i, (src, dst) in enumerate(
            (
                (wg_hbm, wg),
                (wu_hbm, wu),
                (wd_hbm, wd),
                (x_hbm, x.at[own]),
                (cot_hbm, cot.at[own]),
            )
        )
    ]
    for load in loads:
        load.start()

    barrier = pltpu.get_barrier_semaphore()

    @pl.when(has_left)
    def _():
        pl.semaphore_signal(barrier, inc=1, device_id=left_id, device_id_type=MESH)

    @pl.when(has_right)
    def _():
        pl.semaphore_signal(barrier, inc=1, device_id=right_id, device_id_type=MESH)

    for load in small:
        load.wait()
    lead_count = lax.rem(starts_s[0], count)
    row_lead = lax.broadcasted_iota(jnp.int32, (1, count), 1) < lead_count
    scale = combine_v[...].astype(F32).reshape(1, count)
    zero_row = jnp.zeros_like(scale)
    scale_out[...] = jnp.broadcast_to(jnp.where(row_lead, scale, zero_row), scale_out.shape)
    own_col[...] = to_column(jnp.where(row_lead, zero_row, scale))

    @pl.when(has_left & has_right)
    def _():
        pl.semaphore_wait(barrier, 2)

    @pl.when(jnp.logical_not(has_left & has_right))
    def _():
        pl.semaphore_wait(barrier, 1)

    def remote(src, dst, sems, index, peer):
        return pltpu.make_async_remote_copy(
            src_ref=src,
            dst_ref=dst,
            send_sem=sems.at[0, index],
            recv_sem=sems.at[1, index],
            device_id=peer,
            device_id_type=MESH,
        )

    scale_copy = remote(scale_out, scale_in, scale_sem, 0, left_id)
    pieces = count // CHUNK

    def piece(i, base=0):
        return pl.ds(pl.multiple_of(base + i * CHUNK, CHUNK), CHUNK)

    def x_copy(i):
        return remote(x_hbm.at[piece(i)], x.at[piece(i, count)], x_sem, i, left_id)

    def c_copy(i):
        return remote(cot_hbm.at[piece(i)], cot.at[piece(i, count)], c_sem, i, left_id)

    def half_copy(src, dst, sems, i, half):
        at = (piece(i), pl.ds(half * (d // 2), d // 2))
        return remote(src.at[at], dst.at[at], sems, 2 * i + half, right_id)

    def m_copy(i, half):
        return half_copy(send_mixed, back_mixed, m_sem, i, half)

    def i_copy(i, half):
        return half_copy(send_ing, back_ing, i_sem, i, half)

    comb_copy = remote(comb_out, comb_in, comb_sem, 0, right_id)

    @pl.when(has_left)
    def _():
        scale_copy.start()
        for i in range(pieces):
            x_copy(i).start()
        for i in range(pieces):
            c_copy(i).start()

    @pl.when(jnp.logical_not(has_right))
    def _():
        scale_in[...] = jnp.zeros_like(scale_in)
        x[far, :] = jnp.zeros((count, d), BF16)
        cot[far, :] = jnp.zeros((count, d), BF16)

    @pl.when(jnp.logical_not(has_left))
    def _():
        comb_in[...] = jnp.zeros_like(comb_in)
        back_mixed[...] = jnp.zeros_like(back_mixed)
        back_ing[...] = jnp.zeros_like(back_ing)

    def arrive(copy):
        pl.when(has_right)(copy.wait_recv)

    def send_back(copy):
        pl.when(has_right)(copy.start)

    def gate_up(at, gate_ref, up_ref, act_at, spans):
        for cols in spans:
            rows = x[at, :]
            g = dot(rows, wg[:, cols])
            u = dot(rows, wu[:, cols])
            gate_ref[act_at, cols] = g
            up_ref[act_at, cols] = u
            hid[at, cols] = (g * jax.nn.sigmoid(g) * u).astype(BF16)

    def hidden_grads(at, act_at, gate_ref, up_ref):
        for cols in tiles(h, HT):
            hg = dot(og[at, :], wd_t[:, cols])
            g, u = gate_ref[act_at, cols], up_ref[act_at, cols]
            s = jax.nn.sigmoid(g)
            gg[at, cols] = (hg * u * s * (1.0 + g * (1.0 - s))).astype(BF16)
            ug[at, cols] = (hg * (g * s)).astype(BF16)

    def input_grads(at, out_ref, out_at, spans):
        for cols in spans:
            total = dot(gg[at, :], wg_t[:, cols]) + dot(ug[at, :], wu_t[:, cols])
            out_ref[out_at, cols] = total.astype(BF16)

    h_tiles, d_tiles = tiles(h, HT), tiles(d, DT)
    d_halves = d_tiles[: len(d_tiles) // 2], d_tiles[len(d_tiles) // 2 :]

    def far_forward(i):
        at, act_at = piece(i, count), piece(i)
        gate_up(at, far_gate, far_up, act_at, h_tiles)
        for half, spans in enumerate(d_halves):
            for cols in spans:
                out = dot(hid[at, :], wd[:, cols])
                far_out[act_at, cols] = out
                send_mixed[act_at, cols] = (far_col[act_at, 0:1] * out).astype(BF16)
            send_back(m_copy(i, half))

    def far_backward(i):
        at, act_at = piece(i, count), piece(i)
        total = jnp.zeros((CHUNK, 1), F32)
        for cols in d_tiles:
            c = cot[at, cols].astype(F32)
            og[at, cols] = (far_col[act_at, 0:1] * c).astype(BF16)
            total = total + jnp.sum(far_out[act_at, cols] * c, axis=1, keepdims=True)
        far_comb[act_at, :] = jnp.broadcast_to(total, (CHUNK, 128))
        hidden_grads(at, act_at, far_gate, far_up)
        for half, spans in enumerate(d_halves):
            input_grads(at, send_ing, act_at, spans)
            send_back(i_copy(i, half))

    def own_down():
        total = jnp.zeros((count, 1), F32)
        for cols in tiles(d, DT):
            out = dot(hid[own, :], wd[:, cols])
            mixed[:, cols] = (own_col[:, 0:1] * out).astype(BF16)
            c = cot[own, cols].astype(F32)
            og[own, cols] = (own_col[:, 0:1] * c).astype(BF16)
            total = total + jnp.sum(out * c, axis=1, keepdims=True)
        own_comb[...] = jnp.broadcast_to(total, (count, 128))

    def transpose(src, dst):
        for cols in d_tiles:
            dst[:, cols] = src[cols, :].T

    def transpose_down():
        for cols in d_tiles:
            wd_t[cols, :] = wd[:, cols].T

    def own_gate_up(cols):
        gate_up(own, gate, up, own, [cols])

    forward_steps = [functools.partial(own_gate_up, cols) for cols in h_tiles] + [
        own_down,
        functools.partial(transpose, wg, wg_t),
        functools.partial(transpose, wu, wu_t),
        transpose_down,
    ]
    backward_steps = [functools.partial(hidden_grads, own, own, gate, up)] + [
        functools.partial(input_grads, own, ing, own, spans) for spans in d_halves
    ]

    for load in loads:
        load.wait()
    arrive(scale_copy)
    far_col[...] = to_column(scale_in[0:1, :])

    @pl.loop(0, pieces)
    def _(i):
        arrive(x_copy(i))
        far_forward(i)
        for k, step in enumerate(forward_steps):
            pl.when(i == k)(step)

    @pl.loop(0, pieces)
    def _(i):
        arrive(c_copy(i))
        far_backward(i)
        for k, step in enumerate(backward_steps):
            pl.when(i == k)(step)

    comb_out[...] = far_comb[...].T[0 : comb_out.shape[0], :]
    send_back(comb_copy)

    for cols in tiles(d, DT):
        rows = x[:, cols]
        grad_gate[cols, :] = dot_rows(rows, gg[...]).astype(BF16)
        grad_up[cols, :] = dot_rows(rows, ug[...]).astype(BF16)
    for cols in tiles(d, DT):
        grad_down[:, cols] = dot_rows(hid[...], og[:, cols]).astype(BF16)

    def select(copy, back, out, i):
        for half in range(2):
            pl.when(has_left)(copy(i, half).wait_recv)
        lead = lax.broadcasted_iota(jnp.int32, (CHUNK, d), 0) + i * CHUNK < lead_count
        out[piece(i), :] = jnp.where(lead, back[piece(i), :], out[piece(i), :])

    @pl.loop(0, pieces)
    def _(i):
        select(m_copy, back_mixed, mixed, i)

    @pl.loop(0, pieces)
    def _(i):
        select(i_copy, back_ing, ing, i)

    pl.when(has_left)(comb_copy.wait_recv)
    comb[...] = jnp.where(
        jnp.broadcast_to(row_lead, comb.shape), comb_in[...], own_comb[...].T[0 : comb.shape[0], :]
    )

    @pl.when(has_left)
    def _():
        scale_copy.wait_send()
        for i in range(pieces):
            x_copy(i).wait_send()
            c_copy(i).wait_send()

    @pl.when(has_right)
    def _():
        for i in range(pieces):
            for half in range(2):
                m_copy(i, half).wait_send()
                i_copy(i, half).wait_send()
        comb_copy.wait_send()


def exchange(sizes, starts, combine, x, cot, wg, wu, wd):
    count, d = x.shape
    h = wg.shape[1]
    pieces = count // CHUNK
    vmem = pl.BlockSpec(memory_space=pltpu.VMEM)
    dma = pltpu.SemaphoreType.DMA
    return pl.pallas_call(
        functools.partial(exchange_kernel, sizes),
        name="exchange",
        out_shape=(
            jax.ShapeDtypeStruct((count, d), BF16),
            jax.ShapeDtypeStruct((count, d), BF16),
            jax.ShapeDtypeStruct((8, count), F32),
            jax.ShapeDtypeStruct((d, h), BF16),
            jax.ShapeDtypeStruct((d, h), BF16),
            jax.ShapeDtypeStruct((h, d), BF16),
        ),
        in_specs=[pl.BlockSpec(memory_space=pl.ANY)] + [pl.BlockSpec(memory_space=pltpu.HBM)] * 6,
        out_specs=(vmem,) * 6,
        scratch_shapes=[
            pltpu.VMEM((d, h), BF16),
            pltpu.VMEM((d, h), BF16),
            pltpu.VMEM((h, d), BF16),
            pltpu.VMEM((h, d), BF16),
            pltpu.VMEM((h, d), BF16),
            pltpu.VMEM((d, h), BF16),
            pltpu.VMEM((2 * count, d), BF16),
            pltpu.VMEM((2 * count, d), BF16),
            pltpu.VMEM((8, count), F32),
            pltpu.VMEM((8, count), F32),
            pltpu.VMEM((count, 128), F32),
            pltpu.VMEM((count, 128), F32),
            pltpu.VMEM((count, h), F32),
            pltpu.VMEM((count, h), F32),
            pltpu.VMEM((count, h), F32),
            pltpu.VMEM((count, h), F32),
            pltpu.VMEM((count, d), F32),
            pltpu.VMEM((2 * count, h), BF16),
            pltpu.VMEM((2 * count, h), BF16),
            pltpu.VMEM((2 * count, h), BF16),
            pltpu.VMEM((2 * count, d), BF16),
            pltpu.VMEM((count, d), BF16),
            pltpu.VMEM((count, d), BF16),
            pltpu.VMEM((count, d), BF16),
            pltpu.VMEM((count, d), BF16),
            pltpu.VMEM((count, 128), F32),
            pltpu.VMEM((count, 128), F32),
            pltpu.VMEM((8, count), F32),
            pltpu.VMEM((8, count), F32),
            pltpu.SMEM((1,), jnp.int32),
            pltpu.VMEM((count,), BF16),
            dma((7,)),
            dma((2, 1)),
            dma((2, pieces)),
            dma((2, pieces)),
            dma((2, 2 * pieces)),
            dma((2, 2 * pieces)),
            dma((2, 1)),
        ],
        compiler_params=pltpu.CompilerParams(
            collective_id=0, has_side_effects=True, vmem_limit_bytes=40 * 2**20
        ),
    )(starts, *(pltpu.with_memory_space_constraint(a, pltpu.HBM) for a in (combine, x, cot, wg, wu, wd)))


def finish_kernel(mixed, ing, comb, gate, up, down, mixed_o, ing_o, comb_o, gate_o, up_o, down_o, sem):
    copies = [
        pltpu.make_async_copy(src, dst, sem.at[i])
        for i, (src, dst) in enumerate(
            ((gate, gate_o.at[0]), (up, up_o.at[0]), (down, down_o.at[0]), (mixed, mixed_o), (ing, ing_o))
        )
    ]
    for copy in copies:
        copy.start()
    comb_o[...] = comb[0:1, :].reshape(comb_o.shape).astype(BF16)
    for copy in copies:
        copy.wait()


def finish(mixed, ing, comb, gate, up, down):
    anywhere = pl.BlockSpec(memory_space=pl.ANY)
    vmem = pl.BlockSpec(memory_space=pltpu.VMEM)
    return pl.pallas_call(
        finish_kernel,
        name="finish",
        out_shape=(
            jax.ShapeDtypeStruct(mixed.shape, BF16),
            jax.ShapeDtypeStruct(ing.shape, BF16),
            jax.ShapeDtypeStruct(comb.shape[1:], BF16),
            jax.ShapeDtypeStruct((1,) + gate.shape, BF16),
            jax.ShapeDtypeStruct((1,) + up.shape, BF16),
            jax.ShapeDtypeStruct((1,) + down.shape, BF16),
        ),
        in_specs=[vmem] * 6,
        out_specs=(anywhere, anywhere, vmem) + (anywhere,) * 3,
        scratch_shapes=[pltpu.SemaphoreType.DMA((5,))],
        compiler_params=pltpu.CompilerParams(vmem_limit_bytes=2 * 2**20),
    )(*(pltpu.with_memory_space_constraint(a, pltpu.VMEM) for a in (mixed, ing, comb, gate, up, down)))


def solution(mesh):
    sizes = tuple(mesh.shape[axis] for axis in AXES)

    def on_device(sorted_rows, combine, cotangent, starts, w_gate, w_up, w_down):
        mixed, ing, comb, gate, up, down = exchange(
            sizes, starts, combine, sorted_rows, cotangent, w_gate[0], w_up[0], w_down[0]
        )
        mixed, ing, comb, gate, up, down = finish(mixed, ing, comb, gate, up, down)
        return mixed, comb, ing, gate, up, down

    rows2, rows1, rows3 = P(AXES, None), P(AXES), P(AXES, None, None)
    return jax.shard_map(
        on_device,
        mesh=mesh,
        in_specs=(rows2, rows1, rows2, rows1, rows3, rows3, rows3),
        out_specs=(rows2, rows1, rows2, rows3, rows3, rows3),
        check_vma=False,
    )
```

```python
import functools

import jax
import jax.numpy as jnp
from jax import lax
from jax.experimental import pallas as pl
from jax.experimental.pallas import tpu as pltpu
from jax.sharding import PartitionSpec as P

AXES = ("rows", "grp")
MESH = pl.DeviceIdType.MESH
F32 = jnp.float32
BF16 = jnp.bfloat16
CHUNK = 32
HT = 256
DT = 512


def dot(left, right):
    return jnp.dot(left, right, preferred_element_type=F32)


def dot_rows(left, right):
    return lax.dot_general(left, right, (((0,), (0,)), ((), ())), preferred_element_type=F32)


def tiles(extent, width):
    return [pl.ds(lo, width) for lo in range(0, extent, width)]


def to_column(row):
    return jnp.broadcast_to(row, (128, row.shape[1])).T


def exchange_kernel(
    sizes,
    starts, combine, x_hbm, cot_hbm, wg_hbm, wu_hbm, wd_hbm,
    mixed, ing, comb, grad_gate, grad_up, grad_down,
    wg, wu, wd, wg_t, wu_t, wd_t, x, cot, scale_out, scale_in, own_col, far_col,
    gate, up, far_gate, far_up, far_out, hid, gg, ug, og,
    send_mixed, send_ing, back_mixed, back_ing, own_comb, far_comb, comb_out, comb_in,
    starts_s, combine_v, load_sem, scale_sem, x_sem, c_sem, m_sem, i_sem, comb_sem,
):
    n_rows, n_grp = sizes
    last = n_rows * n_grp - 1
    count, d = x_hbm.shape
    h = gate.shape[1]
    own, far = pl.ds(0, count), pl.ds(count, count)
    me = lax.axis_index("rows") * n_grp + lax.axis_index("grp")
    has_left, has_right = me > 0, me < last
    left = lax.rem(me + last, last + 1)
    right = lax.rem(me + 1, last + 1)
    left_id = (left // n_grp, lax.rem(left, n_grp))
    right_id = (right // n_grp, lax.rem(right, n_grp))

    barrier = pltpu.get_barrier_semaphore()

    @pl.when(has_left)
    def _():
        pl.semaphore_signal(barrier, inc=1, device_id=left_id, device_id_type=MESH)

    @pl.when(has_right)
    def _():
        pl.semaphore_signal(barrier, inc=1, device_id=right_id, device_id_type=MESH)

    small = [
        pltpu.make_async_copy(starts, starts_s, load_sem.at[5]),
        pltpu.make_async_copy(combine, combine_v, load_sem.at[6]),
    ]
    for load in small:
        load.start()
    loads = [
        pltpu.make_async_copy(src, dst, load_sem.at[i])
        for i, (src, dst) in enumerate(
            (
                (wg_hbm, wg),
                (wu_hbm, wu),
                (wd_hbm, wd),
                (x_hbm, x.at[own]),
                (cot_hbm, cot.at[own]),
            )
        )
    ]
    for load in loads:
        load.start()

    for load in small:
        load.wait()
    lead_count = lax.rem(starts_s[0], count)
    row_lead = lax.broadcasted_iota(jnp.int32, (1, count), 1) < lead_count
    scale = combine_v[...].astype(F32).reshape(1, count)
    zero_row = jnp.zeros_like(scale)
    scale_out[...] = jnp.broadcast_to(jnp.where(row_lead, scale, zero_row), scale_out.shape)
    own_col[...] = to_column(jnp.where(row_lead, zero_row, scale))

    @pl.when(has_left & has_right)
    def _():
        pl.semaphore_wait(barrier, 2)

    @pl.when(jnp.logical_not(has_left & has_right))
    def _():
        pl.semaphore_wait(barrier, 1)

    def remote(src, dst, sems, index, peer):
        return pltpu.make_async_remote_copy(
            src_ref=src,
            dst_ref=dst,
            send_sem=sems.at[0, index],
            recv_sem=sems.at[1, index],
            device_id=peer,
            device_id_type=MESH,
        )

    scale_copy = remote(scale_out, scale_in, scale_sem, 0, left_id)
    pieces = count // CHUNK

    def piece(i, base=0):
        return pl.ds(pl.multiple_of(base + i * CHUNK, CHUNK), CHUNK)

    def x_copy(i):
        return remote(x_hbm.at[piece(i)], x.at[piece(i, count)], x_sem, i, left_id)

    def c_copy(i):
        return remote(cot_hbm.at[piece(i)], cot.at[piece(i, count)], c_sem, i, left_id)

    def half_copy(src, dst, sems, i, half):
        at = (piece(i), pl.ds(half * (d // 2), d // 2))
        return remote(src.at[at], dst.at[at], sems, 2 * i + half, right_id)

    def m_copy(i, half):
        return half_copy(send_mixed, back_mixed, m_sem, i, half)

    def i_copy(i, half):
        return half_copy(send_ing, back_ing, i_sem, i, half)

    comb_copy = remote(comb_out, comb_in, comb_sem, 0, right_id)

    @pl.when(has_left)
    def _():
        scale_copy.start()
        for i in range(pieces):
            x_copy(i).start()
        for i in range(pieces):
            c_copy(i).start()

    @pl.when(jnp.logical_not(has_right))
    def _():
        scale_in[...] = jnp.zeros_like(scale_in)
        x[far, :] = jnp.zeros((count, d), BF16)
        cot[far, :] = jnp.zeros((count, d), BF16)

    @pl.when(jnp.logical_not(has_left))
    def _():
        comb_in[...] = jnp.zeros_like(comb_in)
        back_mixed[...] = jnp.zeros_like(back_mixed)
        back_ing[...] = jnp.zeros_like(back_ing)

    def arrive(copy):
        pl.when(has_right)(copy.wait_recv)

    def send_back(copy):
        pl.when(has_right)(copy.start)

    def gate_up(at, gate_ref, up_ref, act_at, spans):
        for cols in spans:
            rows = x[at, :]
            g = dot(rows, wg[:, cols])
            u = dot(rows, wu[:, cols])
            gate_ref[act_at, cols] = g
            up_ref[act_at, cols] = u
            hid[at, cols] = (g * jax.nn.sigmoid(g) * u).astype(BF16)

    def hidden_grads(at, act_at, gate_ref, up_ref):
        for cols in tiles(h, HT):
            hg = dot(og[at, :], wd_t[:, cols])
            g, u = gate_ref[act_at, cols], up_ref[act_at, cols]
            s = jax.nn.sigmoid(g)
            gg[at, cols] = (hg * u * s * (1.0 + g * (1.0 - s))).astype(BF16)
            ug[at, cols] = (hg * (g * s)).astype(BF16)

    def input_grads(at, out_ref, out_at, spans):
        for cols in spans:
            total = dot(gg[at, :], wg_t[:, cols]) + dot(ug[at, :], wu_t[:, cols])
            out_ref[out_at, cols] = total.astype(BF16)

    h_tiles, d_tiles = tiles(h, HT), tiles(d, DT)
    d_halves = d_tiles[: len(d_tiles) // 2], d_tiles[len(d_tiles) // 2 :]

    def far_forward(i):
        at, act_at = piece(i, count), piece(i)
        gate_up(at, far_gate, far_up, act_at, h_tiles)
        for half, spans in enumerate(d_halves):
            for cols in spans:
                out = dot(hid[at, :], wd[:, cols])
                far_out[act_at, cols] = out
                send_mixed[act_at, cols] = (far_col[act_at, 0:1] * out).astype(BF16)
            send_back(m_copy(i, half))

    def far_backward(i):
        at, act_at = piece(i, count), piece(i)
        total = jnp.zeros((CHUNK, 1), F32)
        for cols in d_tiles:
            c = cot[at, cols].astype(F32)
            og[at, cols] = (far_col[act_at, 0:1] * c).astype(BF16)
            total = total + jnp.sum(far_out[act_at, cols] * c, axis=1, keepdims=True)
        far_comb[act_at, :] = jnp.broadcast_to(total, (CHUNK, 128))
        hidden_grads(at, act_at, far_gate, far_up)
        for half, spans in enumerate(d_halves):
            input_grads(at, send_ing, act_at, spans)
            send_back(i_copy(i, half))

    def own_down():
        total = jnp.zeros((count, 1), F32)
        for cols in tiles(d, DT):
            out = dot(hid[own, :], wd[:, cols])
            mixed[:, cols] = (own_col[:, 0:1] * out).astype(BF16)
            c = cot[own, cols].astype(F32)
            og[own, cols] = (own_col[:, 0:1] * c).astype(BF16)
            total = total + jnp.sum(out * c, axis=1, keepdims=True)
        own_comb[...] = jnp.broadcast_to(total, (count, 128))

    def transpose(src, dst):
        for cols in d_tiles:
            dst[:, cols] = src[cols, :].T

    def transpose_down():
        for cols in d_tiles:
            wd_t[cols, :] = wd[:, cols].T

    def own_gate_up(cols):
        gate_up(own, gate, up, own, [cols])

    forward_steps = [functools.partial(own_gate_up, cols) for cols in h_tiles] + [
        own_down,
        functools.partial(transpose, wg, wg_t),
        functools.partial(transpose, wu, wu_t),
        transpose_down,
    ]
    backward_steps = [functools.partial(hidden_grads, own, own, gate, up)] + [
        functools.partial(input_grads, own, ing, own, spans) for spans in d_halves
    ]

    for load in loads:
        load.wait()
    arrive(scale_copy)
    far_col[...] = to_column(scale_in[0:1, :])

    @pl.loop(0, pieces)
    def _(i):
        arrive(x_copy(i))
        far_forward(i)
        for k, step in enumerate(forward_steps):
            pl.when(i == k)(step)

    @pl.loop(0, pieces)
    def _(i):
        arrive(c_copy(i))
        far_backward(i)
        for k, step in enumerate(backward_steps):
            pl.when(i == k)(step)

    comb_out[...] = far_comb[...].T[0 : comb_out.shape[0], :]
    send_back(comb_copy)

    for cols in tiles(d, DT):
        rows = x[:, cols]
        grad_gate[cols, :] = dot_rows(rows, gg[...]).astype(BF16)
        grad_up[cols, :] = dot_rows(rows, ug[...]).astype(BF16)
    for cols in tiles(d, DT):
        grad_down[:, cols] = dot_rows(hid[...], og[:, cols]).astype(BF16)

    def select(copy, back, out, i):
        for half in range(2):
            pl.when(has_left)(copy(i, half).wait_recv)
        lead = lax.broadcasted_iota(jnp.int32, (CHUNK, d), 0) + i * CHUNK < lead_count
        out[piece(i), :] = jnp.where(lead, back[piece(i), :], out[piece(i), :])

    @pl.loop(0, pieces)
    def _(i):
        select(m_copy, back_mixed, mixed, i)

    @pl.when(has_left)
    def _():
        scale_copy.wait_send()
        for i in range(pieces):
            x_copy(i).wait_send()
            c_copy(i).wait_send()

    @pl.when(has_right)
    def _():
        for i in range(pieces):
            for half in range(2):
                m_copy(i, half).wait_send()
                i_copy(i, half).wait_send()
        comb_copy.wait_send()

    comb[...] = own_comb[...].T[0 : comb.shape[0], :]

    @pl.loop(0, pieces)
    def _(i):
        select(i_copy, back_ing, ing, i)

    pl.when(has_left)(comb_copy.wait_recv)
    comb[...] = jnp.where(
        jnp.broadcast_to(row_lead, comb.shape), comb_in[...], comb[...]
    )


def exchange(sizes, starts, combine, x, cot, wg, wu, wd):
    count, d = x.shape
    h = wg.shape[1]
    pieces = count // CHUNK
    vmem = pl.BlockSpec(memory_space=pltpu.VMEM)
    dma = pltpu.SemaphoreType.DMA
    return pl.pallas_call(
        functools.partial(exchange_kernel, sizes),
        name="exchange",
        out_shape=(
            jax.ShapeDtypeStruct((count, d), BF16),
            jax.ShapeDtypeStruct((count, d), BF16),
            jax.ShapeDtypeStruct((8, count), F32),
            jax.ShapeDtypeStruct((d, h), BF16),
            jax.ShapeDtypeStruct((d, h), BF16),
            jax.ShapeDtypeStruct((h, d), BF16),
        ),
        in_specs=[pl.BlockSpec(memory_space=pl.ANY)] + [pl.BlockSpec(memory_space=pltpu.HBM)] * 6,
        out_specs=(vmem,) * 6,
        scratch_shapes=[
            pltpu.VMEM((d, h), BF16),
            pltpu.VMEM((d, h), BF16),
            pltpu.VMEM((h, d), BF16),
            pltpu.VMEM((h, d), BF16),
            pltpu.VMEM((h, d), BF16),
            pltpu.VMEM((d, h), BF16),
            pltpu.VMEM((2 * count, d), BF16),
            pltpu.VMEM((2 * count, d), BF16),
            pltpu.VMEM((8, count), F32),
            pltpu.VMEM((8, count), F32),
            pltpu.VMEM((count, 128), F32),
            pltpu.VMEM((count, 128), F32),
            pltpu.VMEM((count, h), F32),
            pltpu.VMEM((count, h), F32),
            pltpu.VMEM((count, h), F32),
            pltpu.VMEM((count, h), F32),
            pltpu.VMEM((count, d), F32),
            pltpu.VMEM((2 * count, h), BF16),
            pltpu.VMEM((2 * count, h), BF16),
            pltpu.VMEM((2 * count, h), BF16),
            pltpu.VMEM((2 * count, d), BF16),
            pltpu.VMEM((count, d), BF16),
            pltpu.VMEM((count, d), BF16),
            pltpu.VMEM((count, d), BF16),
            pltpu.VMEM((count, d), BF16),
            pltpu.VMEM((count, 128), F32),
            pltpu.VMEM((count, 128), F32),
            pltpu.VMEM((8, count), F32),
            pltpu.VMEM((8, count), F32),
            pltpu.SMEM((1,), jnp.int32),
            pltpu.VMEM((count,), BF16),
            dma((7,)),
            dma((2, 1)),
            dma((2, pieces)),
            dma((2, pieces)),
            dma((2, 2 * pieces)),
            dma((2, 2 * pieces)),
            dma((2, 1)),
        ],
        compiler_params=pltpu.CompilerParams(
            collective_id=0, has_side_effects=True, vmem_limit_bytes=40 * 2**20
        ),
    )(starts, *(pltpu.with_memory_space_constraint(a, pltpu.HBM) for a in (combine, x, cot, wg, wu, wd)))


def finish_kernel(mixed, ing, comb, gate, up, down, mixed_o, ing_o, comb_o, gate_o, up_o, down_o, sem):
    copies = [
        pltpu.make_async_copy(src, dst, sem.at[i])
        for i, (src, dst) in enumerate(
            ((gate, gate_o.at[0]), (up, up_o.at[0]), (down, down_o.at[0]), (mixed, mixed_o), (ing, ing_o))
        )
    ]
    for copy in copies:
        copy.start()
    comb_o[...] = comb[0:1, :].reshape(comb_o.shape).astype(BF16)
    for copy in copies:
        copy.wait()


def finish(mixed, ing, comb, gate, up, down):
    anywhere = pl.BlockSpec(memory_space=pl.ANY)
    vmem = pl.BlockSpec(memory_space=pltpu.VMEM)
    return pl.pallas_call(
        finish_kernel,
        name="finish",
        out_shape=(
            jax.ShapeDtypeStruct(mixed.shape, BF16),
            jax.ShapeDtypeStruct(ing.shape, BF16),
            jax.ShapeDtypeStruct(comb.shape[1:], BF16),
            jax.ShapeDtypeStruct((1,) + gate.shape, BF16),
            jax.ShapeDtypeStruct((1,) + up.shape, BF16),
            jax.ShapeDtypeStruct((1,) + down.shape, BF16),
        ),
        in_specs=[vmem] * 6,
        out_specs=(anywhere, anywhere, vmem) + (anywhere,) * 3,
        scratch_shapes=[pltpu.SemaphoreType.DMA((5,))],
        compiler_params=pltpu.CompilerParams(vmem_limit_bytes=2 * 2**20),
    )(*(pltpu.with_memory_space_constraint(a, pltpu.VMEM) for a in (mixed, ing, comb, gate, up, down)))


def solution(mesh):
    sizes = tuple(mesh.shape[axis] for axis in AXES)

    def on_device(sorted_rows, combine, cotangent, starts, w_gate, w_up, w_down):
        mixed, ing, comb, gate, up, down = exchange(
            sizes, starts, combine, sorted_rows, cotangent, w_gate[0], w_up[0], w_down[0]
        )
        mixed, ing, comb, gate, up, down = finish(mixed, ing, comb, gate, up, down)
        return mixed, comb, ing, gate, up, down

    rows2, rows1, rows3 = P(AXES, None), P(AXES), P(AXES, None, None)
    return jax.shard_map(
        on_device,
        mesh=mesh,
        in_specs=(rows2, rows1, rows2, rows1, rows3, rows3, rows3),
        out_specs=(rows2, rows1, rows2, rows3, rows3, rows3),
        check_vma=False,
    )
```

```python
import functools

import jax
import jax.numpy as jnp
from jax import lax
from jax.experimental import pallas as pl
from jax.experimental.pallas import tpu as pltpu
from jax.sharding import PartitionSpec as P

AXES = ("rows", "grp")
MESH = pl.DeviceIdType.MESH
F32 = jnp.float32
BF16 = jnp.bfloat16
CHUNK = 32
HT = 256
DT = 512


def dot(left, right):
    return jnp.dot(left, right, preferred_element_type=F32)


def dot_rows(left, right):
    return lax.dot_general(left, right, (((0,), (0,)), ((), ())), preferred_element_type=F32)


def tiles(extent, width):
    return [pl.ds(lo, width) for lo in range(0, extent, width)]


def to_column(row):
    return jnp.broadcast_to(row, (128, row.shape[1])).T


def exchange_kernel(
    sizes,
    starts, combine, x_hbm, cot_hbm, wg_hbm, wu_hbm, wd_hbm,
    mixed, ing, comb, grad_gate, grad_up, grad_down,
    wg, wu, wd, wg_t, wu_t, wd_t, x, cot, scale_out, scale_in, own_col, far_col,
    gate, up, far_gate, far_up, far_out, hid, gg, ug, og,
    send_mixed, send_ing, back_mixed, back_ing, own_comb, far_comb, comb_out, comb_in,
    starts_s, combine_v, load_sem, scale_sem, x_sem, c_sem, m_sem, i_sem, comb_sem,
):
    n_rows, n_grp = sizes
    last = n_rows * n_grp - 1
    count, d = x_hbm.shape
    h = gate.shape[1]
    own, far = pl.ds(0, count), pl.ds(count, count)
    me = lax.axis_index("rows") * n_grp + lax.axis_index("grp")
    has_left, has_right = me > 0, me < last
    left = lax.rem(me + last, last + 1)
    right = lax.rem(me + 1, last + 1)
    left_id = (left // n_grp, lax.rem(left, n_grp))
    right_id = (right // n_grp, lax.rem(right, n_grp))

    barrier = pltpu.get_barrier_semaphore()

    @pl.when(has_left)
    def _():
        pl.semaphore_signal(barrier, inc=1, device_id=left_id, device_id_type=MESH)

    @pl.when(has_right)
    def _():
        pl.semaphore_signal(barrier, inc=1, device_id=right_id, device_id_type=MESH)

    small = [
        pltpu.make_async_copy(combine, combine_v, load_sem.at[6]),
    ]
    for load in small:
        load.start()
    loads = [
        pltpu.make_async_copy(src, dst, load_sem.at[i])
        for i, (src, dst) in enumerate(
            (
                (wg_hbm, wg),
                (wu_hbm, wu),
                (wd_hbm, wd),
                (x_hbm, x.at[own]),
                (cot_hbm, cot.at[own]),
            )
        )
    ]
    for load in loads:
        load.start()

    for load in small:
        load.wait()
    lead_count = lax.rem(starts[0:1, 0:1], count)
    row_lead = lax.broadcasted_iota(jnp.int32, (1, count), 1) < lead_count
    scale = combine_v[...].astype(F32).reshape(1, count)
    zero_row = jnp.zeros_like(scale)
    scale_out[...] = jnp.broadcast_to(jnp.where(row_lead, scale, zero_row), scale_out.shape)
    own_col[...] = to_column(jnp.where(row_lead, zero_row, scale))

    @pl.when(has_left & has_right)
    def _():
        pl.semaphore_wait(barrier, 2)

    @pl.when(jnp.logical_not(has_left & has_right))
    def _():
        pl.semaphore_wait(barrier, 1)

    def remote(src, dst, sems, index, peer):
        return pltpu.make_async_remote_copy(
            src_ref=src,
            dst_ref=dst,
            send_sem=sems.at[0, index],
            recv_sem=sems.at[1, index],
            device_id=peer,
            device_id_type=MESH,
        )

    scale_copy = remote(scale_out, scale_in, scale_sem, 0, left_id)
    pieces = count // CHUNK

    def piece(i, base=0):
        return pl.ds(pl.multiple_of(base + i * CHUNK, CHUNK), CHUNK)

    def x_copy(i):
        return remote(x_hbm.at[piece(i)], x.at[piece(i, count)], x_sem, i, left_id)

    def c_copy(i):
        return remote(cot_hbm.at[piece(i)], cot.at[piece(i, count)], c_sem, i, left_id)

    def half_copy(src, dst, sems, i, half):
        at = (piece(i), pl.ds(half * (d // 2), d // 2))
        return remote(src.at[at], dst.at[at], sems, 2 * i + half, right_id)

    def m_copy(i, half):
        return half_copy(send_mixed, back_mixed, m_sem, i, half)

    def i_copy(i, half):
        return half_copy(send_ing, back_ing, i_sem, i, half)

    comb_copy = remote(comb_out, comb_in, comb_sem, 0, right_id)

    @pl.when(has_left)
    def _():
        scale_copy.start()
        for i in range(pieces):
            x_copy(i).start()
        for i in range(pieces):
            c_copy(i).start()

    @pl.when(jnp.logical_not(has_right))
    def _():
        scale_in[...] = jnp.zeros_like(scale_in)
        x[far, :] = jnp.zeros((count, d), BF16)
        cot[far, :] = jnp.zeros((count, d), BF16)

    @pl.when(jnp.logical_not(has_left))
    def _():
        comb_in[...] = jnp.zeros_like(comb_in)
        back_mixed[...] = jnp.zeros_like(back_mixed)
        back_ing[...] = jnp.zeros_like(back_ing)

    def arrive(copy):
        pl.when(has_right)(copy.wait_recv)

    def send_back(copy):
        pl.when(has_right)(copy.start)

    def gate_up(at, gate_ref, up_ref, act_at, spans):
        for cols in spans:
            rows = x[at, :]
            g = dot(rows, wg[:, cols])
            u = dot(rows, wu[:, cols])
            gate_ref[act_at, cols] = g
            up_ref[act_at, cols] = u
            hid[at, cols] = (g * jax.nn.sigmoid(g) * u).astype(BF16)

    def hidden_grads(at, act_at, gate_ref, up_ref):
        for cols in tiles(h, HT):
            hg = dot(og[at, :], wd_t[:, cols])
            g, u = gate_ref[act_at, cols], up_ref[act_at, cols]
            s = jax.nn.sigmoid(g)
            gg[at, cols] = (hg * u * s * (1.0 + g * (1.0 - s))).astype(BF16)
            ug[at, cols] = (hg * (g * s)).astype(BF16)

    def input_grads(at, out_ref, out_at, spans):
        for cols in spans:
            total = dot(gg[at, :], wg_t[:, cols]) + dot(ug[at, :], wu_t[:, cols])
            out_ref[out_at, cols] = total.astype(BF16)

    h_tiles, d_tiles = tiles(h, HT), tiles(d, DT)
    d_halves = d_tiles[: len(d_tiles) // 2], d_tiles[len(d_tiles) // 2 :]

    def far_forward(i):
        at, act_at = piece(i, count), piece(i)
        gate_up(at, far_gate, far_up, act_at, h_tiles)
        for half, spans in enumerate(d_halves):
            for cols in spans:
                out = dot(hid[at, :], wd[:, cols])
                far_out[act_at, cols] = out
                send_mixed[act_at, cols] = (far_col[act_at, 0:1] * out).astype(BF16)
            send_back(m_copy(i, half))

    def far_backward(i):
        at, act_at = piece(i, count), piece(i)
        total = jnp.zeros((CHUNK, 1), F32)
        for cols in d_tiles:
            c = cot[at, cols].astype(F32)
            og[at, cols] = (far_col[act_at, 0:1] * c).astype(BF16)
            total = total + jnp.sum(far_out[act_at, cols] * c, axis=1, keepdims=True)
        far_comb[act_at, :] = jnp.broadcast_to(total, (CHUNK, 128))
        hidden_grads(at, act_at, far_gate, far_up)
        for half, spans in enumerate(d_halves):
            input_grads(at, send_ing, act_at, spans)
            send_back(i_copy(i, half))

    def own_down():
        total = jnp.zeros((count, 1), F32)
        for cols in tiles(d, DT):
            out = dot(hid[own, :], wd[:, cols])
            mixed[:, cols] = (own_col[:, 0:1] * out).astype(BF16)
            c = cot[own, cols].astype(F32)
            og[own, cols] = (own_col[:, 0:1] * c).astype(BF16)
            total = total + jnp.sum(out * c, axis=1, keepdims=True)
        own_comb[...] = jnp.broadcast_to(total, (count, 128))

    def transpose(src, dst):
        for cols in d_tiles:
            dst[:, cols] = src[cols, :].T

    def transpose_down():
        for cols in d_tiles:
            wd_t[cols, :] = wd[:, cols].T

    def own_gate_up(cols):
        gate_up(own, gate, up, own, [cols])

    forward_steps = [functools.partial(own_gate_up, cols) for cols in h_tiles] + [
        own_down,
        functools.partial(transpose, wg, wg_t),
        functools.partial(transpose, wu, wu_t),
        transpose_down,
    ]
    backward_steps = [functools.partial(hidden_grads, own, own, gate, up)] + [
        functools.partial(input_grads, own, ing, own, spans) for spans in d_halves
    ]

    for load in loads:
        load.wait()
    arrive(scale_copy)
    far_col[...] = to_column(scale_in[0:1, :])

    @pl.loop(0, pieces)
    def _(i):
        arrive(x_copy(i))
        far_forward(i)
        for k, step in enumerate(forward_steps):
            pl.when(i == k)(step)

    @pl.loop(0, pieces)
    def _(i):
        arrive(c_copy(i))
        far_backward(i)
        for k, step in enumerate(backward_steps):
            pl.when(i == k)(step)

    comb_out[...] = far_comb[...].T[0 : comb_out.shape[0], :]
    send_back(comb_copy)

    for cols in tiles(d, DT):
        rows = x[:, cols]
        grad_gate[cols, :] = dot_rows(rows, gg[...]).astype(BF16)
        grad_up[cols, :] = dot_rows(rows, ug[...]).astype(BF16)
    for cols in tiles(d, DT):
        grad_down[:, cols] = dot_rows(hid[...], og[:, cols]).astype(BF16)

    def select(copy, back, out, i):
        for half in range(2):
            pl.when(has_left)(copy(i, half).wait_recv)
        lead = lax.broadcasted_iota(jnp.int32, (CHUNK, d), 0) + i * CHUNK < lead_count
        out[piece(i), :] = jnp.where(lead, back[piece(i), :], out[piece(i), :])

    @pl.loop(0, pieces)
    def _(i):
        select(m_copy, back_mixed, mixed, i)

    @pl.when(has_left)
    def _():
        scale_copy.wait_send()
        for i in range(pieces):
            x_copy(i).wait_send()
            c_copy(i).wait_send()

    @pl.when(has_right)
    def _():
        for i in range(pieces):
            for half in range(2):
                m_copy(i, half).wait_send()
                i_copy(i, half).wait_send()
        comb_copy.wait_send()

    comb[...] = own_comb[...].T[0 : comb.shape[0], :]

    @pl.loop(0, pieces)
    def _(i):
        select(i_copy, back_ing, ing, i)

    pl.when(has_left)(comb_copy.wait_recv)
    comb[...] = jnp.where(
        jnp.broadcast_to(row_lead, comb.shape), comb_in[...], comb[...]
    )


def exchange(sizes, starts, combine, x, cot, wg, wu, wd):
    count, d = x.shape
    h = wg.shape[1]
    pieces = count // CHUNK
    vmem = pl.BlockSpec(memory_space=pltpu.VMEM)
    dma = pltpu.SemaphoreType.DMA
    return pl.pallas_call(
        functools.partial(exchange_kernel, sizes),
        name="exchange",
        out_shape=(
            jax.ShapeDtypeStruct((count, d), BF16),
            jax.ShapeDtypeStruct((count, d), BF16),
            jax.ShapeDtypeStruct((8, count), F32),
            jax.ShapeDtypeStruct((d, h), BF16),
            jax.ShapeDtypeStruct((d, h), BF16),
            jax.ShapeDtypeStruct((h, d), BF16),
        ),
        in_specs=[vmem] + [pl.BlockSpec(memory_space=pltpu.HBM)] * 6,
        out_specs=(vmem,) * 6,
        scratch_shapes=[
            pltpu.VMEM((d, h), BF16),
            pltpu.VMEM((d, h), BF16),
            pltpu.VMEM((h, d), BF16),
            pltpu.VMEM((h, d), BF16),
            pltpu.VMEM((h, d), BF16),
            pltpu.VMEM((d, h), BF16),
            pltpu.VMEM((2 * count, d), BF16),
            pltpu.VMEM((2 * count, d), BF16),
            pltpu.VMEM((8, count), F32),
            pltpu.VMEM((8, count), F32),
            pltpu.VMEM((count, 128), F32),
            pltpu.VMEM((count, 128), F32),
            pltpu.VMEM((count, h), F32),
            pltpu.VMEM((count, h), F32),
            pltpu.VMEM((count, h), F32),
            pltpu.VMEM((count, h), F32),
            pltpu.VMEM((count, d), F32),
            pltpu.VMEM((2 * count, h), BF16),
            pltpu.VMEM((2 * count, h), BF16),
            pltpu.VMEM((2 * count, h), BF16),
            pltpu.VMEM((2 * count, d), BF16),
            pltpu.VMEM((count, d), BF16),
            pltpu.VMEM((count, d), BF16),
            pltpu.VMEM((count, d), BF16),
            pltpu.VMEM((count, d), BF16),
            pltpu.VMEM((count, 128), F32),
            pltpu.VMEM((count, 128), F32),
            pltpu.VMEM((8, count), F32),
            pltpu.VMEM((8, count), F32),
            pltpu.SMEM((1,), jnp.int32),
            pltpu.VMEM((count,), BF16),
            dma((7,)),
            dma((2, 1)),
            dma((2, pieces)),
            dma((2, pieces)),
            dma((2, 2 * pieces)),
            dma((2, 2 * pieces)),
            dma((2, 1)),
        ],
        compiler_params=pltpu.CompilerParams(
            collective_id=0, has_side_effects=True, vmem_limit_bytes=40 * 2**20
        ),
    )(jnp.broadcast_to(starts, (8, 128)), *(pltpu.with_memory_space_constraint(a, pltpu.HBM) for a in (combine, x, cot, wg, wu, wd)))


def finish_kernel(mixed, ing, comb, gate, up, down, mixed_o, ing_o, comb_o, gate_o, up_o, down_o, sem):
    copies = [
        pltpu.make_async_copy(src, dst, sem.at[i])
        for i, (src, dst) in enumerate(
            ((gate, gate_o.at[0]), (up, up_o.at[0]), (down, down_o.at[0]), (mixed, mixed_o), (ing, ing_o))
        )
    ]
    for copy in copies:
        copy.start()
    comb_o[...] = comb[0:1, :].reshape(comb_o.shape).astype(BF16)
    for copy in copies:
        copy.wait()


def finish(mixed, ing, comb, gate, up, down):
    anywhere = pl.BlockSpec(memory_space=pl.ANY)
    vmem = pl.BlockSpec(memory_space=pltpu.VMEM)
    return pl.pallas_call(
        finish_kernel,
        name="finish",
        out_shape=(
            jax.ShapeDtypeStruct(mixed.shape, BF16),
            jax.ShapeDtypeStruct(ing.shape, BF16),
            jax.ShapeDtypeStruct(comb.shape[1:], BF16),
            jax.ShapeDtypeStruct((1,) + gate.shape, BF16),
            jax.ShapeDtypeStruct((1,) + up.shape, BF16),
            jax.ShapeDtypeStruct((1,) + down.shape, BF16),
        ),
        in_specs=[vmem] * 6,
        out_specs=(anywhere, anywhere, vmem) + (anywhere,) * 3,
        scratch_shapes=[pltpu.SemaphoreType.DMA((5,))],
        compiler_params=pltpu.CompilerParams(vmem_limit_bytes=2 * 2**20),
    )(*(pltpu.with_memory_space_constraint(a, pltpu.VMEM) for a in (mixed, ing, comb, gate, up, down)))


def solution(mesh):
    sizes = tuple(mesh.shape[axis] for axis in AXES)

    def on_device(sorted_rows, combine, cotangent, starts, w_gate, w_up, w_down):
        mixed, ing, comb, gate, up, down = exchange(
            sizes, starts, combine, sorted_rows, cotangent, w_gate[0], w_up[0], w_down[0]
        )
        mixed, ing, comb, gate, up, down = finish(mixed, ing, comb, gate, up, down)
        return mixed, comb, ing, gate, up, down

    rows2, rows1, rows3 = P(AXES, None), P(AXES), P(AXES, None, None)
    return jax.shard_map(
        on_device,
        mesh=mesh,
        in_specs=(rows2, rows1, rows2, rows1, rows3, rows3, rows3),
        out_specs=(rows2, rows1, rows2, rows3, rows3, rows3),
        check_vma=False,
    )
```
